128 devices in a mesh: img: 8 (over y, z_lo), ori: 16 (over z_hi, x, core).
Axes of the slice: x: 4, y: 4, z: 4 (z_hi: 2, z_lo: 2; z = z_hi * 2 + z_lo), core: 2. Of those that a mesh axis runs over, the one named last changes fastest.
Arguments:
- images: bfloat16 [2048, 2, 8192], P('img'), may hold values from -24 to 24
- projections: bfloat16 [2048, 2, 8192], P('ori'), may hold values from -0.2421875 to 0.2421875
- noise_weight: float32 [8192], replicated, may hold values from 0.25 to 4
- shift_ids: int32 [2048, 4], P('img'), may hold values from 0 to 48
- owner_ids: int32 [2048, 64], P('ori', 'img'), may hold values from 0 to 127, as said below
- cell_ids: int32 [2048, 64], P('ori', 'img'), may hold values from 0 to 1023
- weight_ids: int32 [2048, 64], P('ori', 'img'), may hold values from 0 to 63
- interp_table: bfloat16 [64, 128, 128], replicated, may hold values from -0.5 to 0.5
Outputs:
- realspace: float32 [2, 256, 256, 256], P(None, 'img', 'ori')
- loglik: float32 [2048], P('img')
The draws below stay inside these ranges and needn't reach their ends.
Inputs may be any that keep to these rules, and one draw needn't show every extreme that they name: `owner_ids`: among the blocks of one device (rows of one index of ori, columns of one index of img), at most 24 name any one owner; one owner is named exactly 24 times by the blocks of every device.
All inputs are finite; a program needn't handle non-finite values.
Results may differ from the reference program's by a relative error of at most 0.0058.
Values may be sent and summed in bfloat16 or wider, within the bound.
No kernel may reach another device: no remote copies, remote signals or barrier semaphores. Data moves between devices by JAX's collectives and lax.ppermute only.
A program may use at most 192 MiB of HBM per device.

```python
import math
import jax
import jax.numpy as jnp
from jax import lax

IMGBOX = 128
K = 8192
LB = 128
BOX = 256
SHIFTS = 4
NTRANS = 49
NWB = 64
ORI_DEV = 128
IMAGES = 2048
ORIENT = 2048
CBLK = 64
CB_DEV = 8
CAP = 24
X_DEV = 16
Y_DEV = 32
ZB = 2
CELLB = 1024
N_IMG = 8
N_ORI = 16
DEVICES = 128


def draw_shared(key):
    shift_table = jax.random.randint(jax.random.fold_in(key, 11), (IMAGES, SHIFTS), 0, NTRANS)
    subkeys = jax.random.split(jax.random.fold_in(key, 12), 3)
    noise_table = jnp.exp(jax.random.uniform(subkeys[0], (K,), jnp.float32, math.log(0.25), math.log(4.0)))
    base_scale = 2.0 / math.sqrt(2 * K)
    image_scale = 0.35
    rising = 0.4 + 0.45 * jnp.arange(ORIENT, dtype=jnp.float32) / max(ORIENT - 1, 1)
    proj_table = jnp.clip(jax.random.normal(subkeys[1], (ORIENT, 2, K), jnp.float32), -4.0, 4.0)
    image_table = jnp.clip(jax.random.normal(subkeys[2], (IMAGES, 2, K), jnp.float32), -4.0, 4.0)
    image_rows = jnp.ones((IMAGES,), jnp.float32)
    proj_table = proj_table * (base_scale * rising)[:, None, None]
    image_table = image_table * (image_scale * image_rows)[:, None, None]
    return (image_table, proj_table, noise_table, shift_table)


def draw_images(key, part):
    return draw_shared(key)[0].astype(jnp.bfloat16)


def draw_projections(key, part):
    return draw_shared(key)[1].astype(jnp.bfloat16)


def draw_noise_weight(key, part):
    return draw_shared(key)[2].astype(jnp.float32)


def draw_shift_ids(key, part):
    return draw_shared(key)[3].astype(jnp.int32)


def draw_owner_ids(key, part):
    slot_count = DEVICES * CAP
    per_device = ORI_DEV * CB_DEV
    boosts = jax.random.randint(jax.random.fold_in(key, 21), (DEVICES,), 0, 4096)
    ranked = boosts * DEVICES + jnp.arange(DEVICES, dtype=jnp.int32)
    favoured = jnp.argmax(ranked)

    def one_source(source):
        source_key = jax.random.fold_in(jax.random.fold_in(key, 22), source)
        noise_int = jax.random.randint(source_key, (DEVICES, CAP), 0, 4096)
        scores = boosts[:, None] * 2 + noise_int
        scores = scores * slot_count + jnp.arange(slot_count, dtype=jnp.int32).reshape(DEVICES, CAP)
        forced = jnp.where(jnp.arange(DEVICES) == favoured, 1073741824, 0).astype(jnp.int32)
        scores = scores + forced[:, None]
        unused, chosen = lax.top_k(scores.reshape(-1), per_device)
        owners = chosen // CAP
        shuffle = jax.random.permutation(jax.random.fold_in(source_key, 1), per_device)
        return owners[shuffle].reshape(ORI_DEV, CB_DEV)
    owner_table = jax.vmap(one_source)(jnp.arange(DEVICES, dtype=jnp.int32))
    owner_table = owner_table.reshape(N_IMG, N_ORI, ORI_DEV, CB_DEV).transpose(1, 2, 0, 3)
    return owner_table.reshape(ORIENT, CBLK).astype(jnp.int32)


def plant(array, rng, smallest, largest):
    spot = [jax.random.randint(jax.random.fold_in(rng, axis), (), 0, length) for axis, length in enumerate(array.shape)]
    longest = array.shape.index(max(array.shape))
    next_to = spot[:longest] + [(spot[longest] + 1) % array.shape[longest]] + spot[longest + 1:]
    return array.at[tuple(spot)].set(smallest).at[tuple(next_to)].set(largest)


def centred(key, dims, width, reach, kind=jnp.bfloat16):
    return jnp.clip(width * jax.random.normal(key, dims, jnp.float32), -reach, reach).astype(kind)


def setup_inputs(seed: int = 0) -> dict:
    streams_of = jax.random.split(jax.random.key(seed), 9)
    return {
        "images": draw_images(jax.random.fold_in(streams_of[8], 71), 0),
        "projections": draw_projections(jax.random.fold_in(streams_of[8], 71), 0),
        "noise_weight": draw_noise_weight(jax.random.fold_in(streams_of[8], 71), 0),
        "shift_ids": draw_shift_ids(jax.random.fold_in(streams_of[8], 71), 0),
        "owner_ids": draw_owner_ids(jax.random.fold_in(streams_of[8], 71), 0),
        "cell_ids": plant(jax.random.randint(streams_of[5], (ORIENT, CBLK), 0, CELLB), jax.random.fold_in(streams_of[5], 1), 0, CELLB - 1).astype(jnp.int32),
        "weight_ids": plant(jax.random.randint(streams_of[6], (ORIENT, CBLK), 0, NWB), jax.random.fold_in(streams_of[6], 1), 0, NWB - 1).astype(jnp.int32),
        "interp_table": centred(streams_of[7], (NWB, LB, LB), LB ** -0.5, 0.5),
    }


def phase_parts(shift_list):
    coef = jnp.arange(K, dtype=jnp.int32)
    kx_index = coef % IMGBOX - IMGBOX // 2
    ky_index = coef // IMGBOX
    shift_x = shift_list % 7 - 3
    shift_y = shift_list // 7 - 3
    phase_turns = (kx_index[None, :] * shift_x[:, None] + ky_index[None, :] * shift_y[:, None]) % IMGBOX
    angles = phase_turns.astype(jnp.float32) * (-2.0 * math.pi / IMGBOX)
    return jnp.cos(angles), jnp.sin(angles)


def aligned_rows(images, shift_ids):
    row_count = images.shape[0]
    cosine, sine_table = phase_parts(shift_ids.reshape(-1).astype(jnp.int32))
    cosine = cosine.reshape(row_count, SHIFTS, K)
    sine_table = sine_table.reshape(row_count, SHIFTS, K)
    real_part = images[:, 0, :].astype(jnp.float32)[:, None, :]
    imag_part = images[:, 1, :].astype(jnp.float32)[:, None, :]
    new_real = real_part * cosine - imag_part * sine_table
    new_imag = real_part * sine_table + imag_part * cosine
    stacked = jnp.stack([new_real, new_imag], axis=2).astype(jnp.bfloat16)
    return stacked.reshape(row_count * SHIFTS, 2 * K)


def reference(images, projections, noise_weight, shift_ids, owner_ids, cell_ids, weight_ids, interp_table):
    aligned = aligned_rows(images, shift_ids)
    proj_float = projections.astype(jnp.float32)
    weighted = (proj_float * noise_weight).astype(jnp.bfloat16).reshape(ORIENT, 2 * K)
    pnorm = jnp.sum(proj_float * proj_float * noise_weight, axis=(1, 2))
    scores = lax.dot_general(aligned, weighted, (((1,), (1,)), ((), ())), preferred_element_type=jnp.float32)
    scores = scores.reshape(IMAGES, SHIFTS, ORIENT) - 0.5 * pnorm
    row_peak = jnp.max(scores, axis=(1, 2))
    row_total = jnp.sum(jnp.exp(scores - row_peak[:, None, None]), axis=(1, 2))
    loglik = row_peak + jnp.log(row_total)
    weights_bf = (jnp.exp(scores - row_peak[:, None, None]) / row_total[:, None, None]).astype(jnp.bfloat16)
    weights_bf = weights_bf.reshape(IMAGES * SHIFTS, ORIENT)
    slices = lax.dot_general(weights_bf, aligned, (((0,), (0,)), ((), ())), preferred_element_type=jnp.float32)
    slices = slices.astype(jnp.bfloat16).reshape(ORIENT, 2, CBLK, LB).transpose(0, 2, 1, 3)

    def block_terms(entries):
        block_values, table_ids = entries
        picked = interp_table[table_ids].astype(jnp.float32)
        return jnp.einsum('cpk,ckj->cpj', block_values.astype(jnp.float32), picked, precision=lax.Precision.HIGHEST)

    contribution = lax.map(block_terms, (slices, weight_ids.astype(jnp.int32)))
    img_index = owner_ids // N_ORI
    ori_index = owner_ids % N_ORI
    pencil = cell_ids // ZB
    half_index = cell_ids % ZB
    x_pos = ori_index * X_DEV + pencil // Y_DEV
    y_pos = img_index * Y_DEV + pencil % Y_DEV
    base_index = (x_pos * BOX + y_pos) * BOX + half_index * LB
    flat_index = (base_index[:, :, None] + jnp.arange(LB, dtype=jnp.int32)[None, None, :]).astype(jnp.int32)
    volume = jnp.zeros((2, BOX * BOX * BOX), jnp.float32)
    volume = volume.at[0, flat_index].add(contribution[:, :, 0, :])
    volume = volume.at[1, flat_index].add(contribution[:, :, 1, :])
    volume = volume.reshape(2, BOX, BOX, BOX)
    transformed = jnp.fft.ifftn(volume[0] + 1j * volume[1], norm="ortho")
    real_out = jnp.transpose(jnp.real(transformed), (2, 1, 0)).astype(jnp.float32)
    imag_out = jnp.transpose(jnp.imag(transformed), (2, 1, 0)).astype(jnp.float32)
    realspace = jnp.stack([real_out, imag_out])
    return realspace, loglik
```

```python
import math

import jax
import jax.numpy as jnp
import ml_dtypes
import numpy as np
from jax import lax
from jax.experimental import pallas as pl
from jax.experimental.pallas import tpu as pltpu
from jax.sharding import PartitionSpec as P

BF = jnp.bfloat16
F32 = jnp.float32
I32 = jnp.int32

IB = 32
STRIDE = 136
CAP = 24
VMEM_LIMIT = 56 * 1024 * 1024


def split_np(a):
    high = a.astype(ml_dtypes.bfloat16)
    low = (a - high.astype(np.float64)).astype(ml_dtypes.bfloat16)
    return high, low


def dft_np():
    k = np.arange(256)
    ang = 2.0 * math.pi * ((k[:, None] * k[None, :]) % 256) / 256.0
    return np.cos(ang) / 16.0, np.sin(ang) / 16.0


def dot(a, b):
    return lax.dot_general(a, b, (((1,), (0,)), ((), ())), preferred_element_type=F32)


def split(a):
    high = a.astype(BF)
    return high, (a - high.astype(F32)).astype(BF)


def align_kernel(x_ref, pr_ref, nw_ref, sh_ref, ex_ref, a_ref, sc_ref, st_ref,
                 xf, wk, pn, ph, stp):
    b = pl.program_id(0)

    @pl.when(b == 0)
    def _():
        def chunk(oc, carry):
            def load(i, c2):
                xf[pl.ds(pl.multiple_of(i * STRIDE, 8), 128), :] = pr_ref[oc * IB + i].astype(F32)
                return c2
            lax.fori_loop(0, IB, load, 0, unroll=4)
            rows = pl.ds(pl.multiple_of(oc * IB, IB), IB)

            def ky_step(ky, acc):
                noise = nw_ref[pl.ds(ky, 1), :]
                for p in range(2):
                    v = xf[pl.ds(2 * ky + p, IB, stride=STRIDE), :]
                    vn = v * noise
                    wk[rows, pl.ds(pl.multiple_of(ky * 256 + p * 128, 128), 128)] = vn.astype(BF)
                    acc = acc + v * vn
                return acc
            acc = lax.fori_loop(0, 64, ky_step, jnp.zeros((IB, 128), F32), unroll=4)
            pn[rows, :] = jnp.broadcast_to(jnp.sum(acc, axis=1, keepdims=True) * 0.5, (IB, 128))
            return carry
        lax.fori_loop(0, 128 // IB, chunk, 0)

    def load(i, c2):
        xf[pl.ds(pl.multiple_of(i * STRIDE, 8), 128), :] = x_ref[i].astype(F32)
        return c2
    lax.fori_loop(0, IB, load, 0, unroll=4)

    for s in range(4):
        t = sh_ref[:, s:s + 1]
        ty = (t * 37) >> 8
        tx = t - ty * 7
        er = jnp.zeros((IB, 128), F32)
        ei = jnp.zeros((IB, 128), F32)
        sr = jnp.zeros((IB, 1), F32)
        si = jnp.zeros((IB, 1), F32)
        for d in range(7):
            hit = tx == d
            er = jnp.where(hit, ex_ref[d:d + 1, :], er)
            ei = jnp.where(hit, ex_ref[8 + d:9 + d, :], ei)
            ang = -2.0 * math.pi * (d - 3) / 128.0
            hity = ty == d
            sr = jnp.where(hity, math.cos(ang), sr)
            si = jnp.where(hity, math.sin(ang), si)
        ph[0, s] = er
        ph[1, s] = ei
        stp[0, s] = jnp.broadcast_to(sr, (IB, 128))
        stp[1, s] = jnp.broadcast_to(si, (IB, 128))

    def kchunk(kc, acc):
        for s in range(4):
            pr = ph[0, s]
            pi = ph[1, s]
            sr = stp[0, s]
            si = stp[1, s]
            for j in range(8):
                ky = kc * 8 + j
                re = xf[pl.ds(2 * ky, IB, stride=STRIDE), :]
                im = xf[pl.ds(2 * ky + 1, IB, stride=STRIDE), :]
                lane = pl.multiple_of(ky * 256, 256)
                a_ref[s * IB:(s + 1) * IB, pl.ds(lane, 128)] = (re * pr - im * pi).astype(BF)
                a_ref[s * IB:(s + 1) * IB, pl.ds(lane + 128, 128)] = (re * pi + im * pr).astype(BF)
                pr, pi = pr * sr - pi * si, pr * si + pi * sr
            ph[0, s] = pr
            ph[1, s] = pi
        lanes = pl.ds(pl.multiple_of(kc * 2048, 2048), 2048)
        return acc + lax.dot_general(wk[:, lanes], a_ref[:, lanes], (((1,), (1,)), ((), ())),
                                     preferred_element_type=F32)
    acc = lax.fori_loop(0, 8, kchunk, jnp.zeros((128, 4 * IB), F32))
    sc = acc - pn[...]
    sc_ref[0] = sc
    mx = jnp.max(sc, axis=0, keepdims=True)
    mx = jnp.maximum(mx, pltpu.roll(mx, 64, 1))
    mx = jnp.maximum(mx, pltpu.roll(mx, 32, 1))
    tot = jnp.sum(jnp.exp(sc - mx), axis=0, keepdims=True)
    tot = tot + pltpu.roll(tot, 64, 1)
    tot = tot + pltpu.roll(tot, 32, 1)
    st_ref[0, pl.ds(b, 1), :] = mx
    st_ref[1, pl.ds(b, 1), :] = tot


def align_call(xv, pv, noise, shifts):
    n_img = xv.shape[0]
    steps = n_img // IB
    kx = np.arange(128) - 64
    ex = np.zeros((16, 128), np.float32)
    for d in range(7):
        ang = -2.0 * math.pi * ((kx * (d - 3)) % 128) / 128.0
        ex[d] = np.cos(ang)
        ex[8 + d] = np.sin(ang)
    whole3 = lambda b: (0, 0, 0)
    whole2 = lambda b: (0, 0)
    return pl.pallas_call(
        align_kernel,
        grid=(steps,),
        in_specs=[
            pl.BlockSpec((IB, 128, 128), lambda b: (b, 0, 0)),
            pl.BlockSpec((128, 128, 128), whole3, pipeline_mode=pl.Buffered(1)),
            pl.BlockSpec((64, 128), whole2),
            pl.BlockSpec((IB, 4), lambda b: (b, 0)),
            pl.BlockSpec((16, 128), whole2),
        ],
        out_specs=[
            pl.BlockSpec((4 * IB, 16384), lambda b: (b, 0)),
            pl.BlockSpec((1, 128, 4 * IB), lambda b: (b, 0, 0)),
            pl.BlockSpec((2, steps, 128), whole3),
        ],
        out_shape=[
            jax.ShapeDtypeStruct((4 * n_img, 16384), BF),
            jax.ShapeDtypeStruct((steps, 128, 4 * IB), F32),
            jax.ShapeDtypeStruct((2, steps, 128), F32),
        ],
        scratch_shapes=[
            pltpu.VMEM((IB * STRIDE, 128), F32),
            pltpu.VMEM((128, 16384), BF),
            pltpu.VMEM((128, 128), F32),
            pltpu.VMEM((2, 4, IB, 128), F32),
            pltpu.VMEM((2, 4, IB, 128), F32),
        ],
        compiler_params=pltpu.CompilerParams(vmem_limit_bytes=VMEM_LIMIT),
        name="align_scores",
    )(xv, pv, noise, shifts, jnp.asarray(ex))


def slices_kernel(sc_ref, st_ref, a_ref, out_ref, ll_ref, pt):
    @pl.when(pl.program_id(0) == 0)
    def _():
        n = st_ref.shape[0]
        peak = st_ref[0, 0]
        for q in range(1, n):
            peak = jnp.maximum(peak, st_ref[q, 0])
        total = jnp.zeros_like(peak)
        for q in range(n):
            total = total + st_ref[q, 1] * jnp.exp(st_ref[q, 0] - peak)
        ll_ref[...] = peak + jnp.log(total)
        inv = 1.0 / total
        for blk in range(sc_ref.shape[0]):
            pr = jnp.exp(sc_ref[blk] - peak[blk:blk + 1, :]) * inv[blk:blk + 1, :]
            pt[:, blk * 128:(blk + 1) * 128] = pr.astype(BF)
    out_ref[0] = dot(pt[...], a_ref[...]).astype(BF)


def slices_call(sc, st, a):
    rows = a.shape[0]
    steps = sc.shape[0]
    return pl.pallas_call(
        slices_kernel,
        grid=(8,),
        in_specs=[
            pl.BlockSpec(sc.shape, lambda r: (0, 0, 0)),
            pl.BlockSpec(st.shape, lambda r: (0, 0, 0, 0)),
            pl.BlockSpec((rows, 2048), lambda r: (0, r)),
        ],
        out_specs=[
            pl.BlockSpec((1, 128, 2048), lambda r: (r, 0, 0)),
            pl.BlockSpec((steps, 128), lambda r: (0, 0)),
        ],
        out_shape=[
            jax.ShapeDtypeStruct((8, 128, 2048), BF),
            jax.ShapeDtypeStruct((steps, 128), F32),
        ],
        scratch_shapes=[pltpu.VMEM((128, rows), BF)],
        compiler_params=pltpu.CompilerParams(vmem_limit_bytes=VMEM_LIMIT),
        name="slice_sums",
    )(sc, st, a)


def slots_kernel(ow_ref, ce_ref, slot_ref, cell_ref):
    lane = lax.broadcasted_iota(I32, (128, 128), 1)
    sub = lax.broadcasted_iota(I32, (128, 128), 0)
    lower = (sub >= lane).astype(F32).astype(BF)
    base = jnp.zeros((1, 128), F32)
    slot_all = jnp.zeros((128, 128), F32)
    cell_all = jnp.zeros((128, 128), F32)
    columns = []
    for c in range(8):
        oc = ow_ref[:, c:c + 1]
        hit = (oc == lane).astype(F32)
        run = dot(lower, hit.astype(BF)) + base
        rank = jnp.sum(run * hit, axis=1, keepdims=True) - 1.0
        base = base + jnp.sum(hit, axis=0, keepdims=True)
        slot = oc.astype(F32) * float(CAP) + rank
        columns.append(slot.astype(I32))
        slot_all = jnp.where(lane == c, slot, slot_all)
        cell_all = jnp.where(lane == c, ce_ref[:, c:c + 1].astype(F32), cell_all)
    slot_ref[...] = jnp.transpose(slot_all)[0:8, :].astype(I32)
    cells_t = jnp.transpose(cell_all)[0:8, :]
    high = jnp.floor(cells_t * (1.0 / 32.0))
    low = cells_t - high * 32.0
    row = lax.broadcasted_iota(I32, (16, 128), 0)
    n_slot = cell_ref.shape[1]
    slot_lane = lax.broadcasted_iota(I32, (128, n_slot), 1)
    acc = jnp.zeros((16, n_slot), F32)
    for c in range(8):
        parts = jnp.where(row == 0, high[c:c + 1, :],
                          jnp.where(row == 1, low[c:c + 1, :], jnp.where(row == 2, 1.0, 0.0)))
        pick = (columns[c] == slot_lane).astype(F32).astype(BF)
        acc = acc + dot(parts.astype(BF), pick)
    cell = acc[0:1, :] * 32.0 + acc[1:2, :]
    cell_ref[...] = jnp.where(acc[2:3, :] > 0.5, cell, -1.0).astype(I32)


def slots_call(owners, cells, n_slot):
    return pl.pallas_call(
        slots_kernel,
        out_shape=[jax.ShapeDtypeStruct((8, 128), I32), jax.ShapeDtypeStruct((1, n_slot), I32)],
        compiler_params=pltpu.CompilerParams(vmem_limit_bytes=VMEM_LIMIT),
        name="slots",
    )(owners, cells)


WSTEP = 4


def interp_kernel(r0_ref, wid_ref, slot_ref, tab_ref, out_ref, blk, tid, acc, con):
    for c in range(8):
        tid[c * 128:(c + 1) * 128, :] = jnp.broadcast_to(wid_ref[:, c:c + 1], (128, 128))
        for p in range(2):
            lanes = slice(c * 256 + p * 128, c * 256 + (p + 1) * 128)
            total = r0_ref[0, :, lanes].astype(F32)
            for q in range(1, 8):
                total = total + r0_ref[q, :, lanes].astype(F32)
            blk[p * 1024 + c * 128:p * 1024 + (c + 1) * 128, :] = total.astype(BF).astype(F32)
    acc[...] = jnp.zeros_like(acc)

    def step(g, carry):
        table = tab_ref[pl.ds(pl.multiple_of(g * (WSTEP * 128), WSTEP * 128), WSTEP * 128), :]
        for half in range(8):
            rows = slice(half * 256, (half + 1) * 256)
            trow = slice((half % 4) * 256, (half % 4 + 1) * 256)
            values = blk[rows, :]
            ids = tid[trow, :]
            lhs = jnp.concatenate(
                [jnp.where(ids == g * WSTEP + u, values, 0.0).astype(BF) for u in range(WSTEP)], axis=1)
            acc[rows, :] += dot(lhs, table)
        return carry
    lax.fori_loop(0, 64 // WSTEP, step, 0)
    con[:, 0:128] = acc[0:1024, :].astype(BF)
    con[:, 128:256] = acc[1024:2048, :].astype(BF)

    def place(k, carry):
        row = lax.broadcasted_iota(I32, (384, 128), 0) + k * 384
        pick = jnp.concatenate(
            [jnp.where(slot_ref[c:c + 1, :] == row, 1.0, 0.0).astype(BF) for c in range(8)], axis=1)
        out_ref[pl.ds(pl.multiple_of(k * 384, 384), 384), :] = dot(pick, con[...]).astype(BF)
        return carry
    lax.fori_loop(0, out_ref.shape[0] // 384, place, 0)


def interp_call(r0, wid, slots, table, n_slot):
    return pl.pallas_call(
        interp_kernel,
        out_shape=jax.ShapeDtypeStruct((n_slot, 256), BF),
        scratch_shapes=[
            pltpu.VMEM((2048, 128), F32),
            pltpu.VMEM((1024, 128), I32),
            pltpu.VMEM((2048, 128), F32),
            pltpu.VMEM((1024, 256), BF),
        ],
        compiler_params=pltpu.CompilerParams(vmem_limit_bytes=VMEM_LIMIT),
        name="interpolate",
    )(r0, wid, slots, table)


def volume_kernel(rv_ref, cell_ref, dh_ref, dl_ref, out_ref, vol):
    n_slot = rv_ref.shape[0]
    cell = cell_ref[...]
    half = cell & 1
    y = (cell >> 1) & 31
    x = cell >> 6
    where = half * 512 + (x & 1) * 256 + (x >> 1) * 32 + y
    where = jnp.where(cell < 0, -1, where)

    def land(k, carry):
        row = lax.broadcasted_iota(I32, (128, n_slot), 0) + k * 128
        pick = jnp.where(where == row, 1.0, 0.0).astype(BF)
        vol[pl.ds(pl.multiple_of(k * 128, 128), 128), :] = dot(pick, rv_ref[...])
        return carry
    lax.fori_loop(0, 8, land, 0)
    lane = lax.broadcasted_iota(I32, (256, 128), 1)
    outs = []
    for xl in range(2):
        lo = slice(xl * 256, (xl + 1) * 256)
        hi = slice(512 + xl * 256, 512 + (xl + 1) * 256)
        field = jnp.concatenate(
            [vol[lo, 0:128], vol[hi, 0:128], vol[lo, 128:256], vol[hi, 128:256]], axis=1)
        fh, fl = split(field)
        outs.append(dot(fh, dh_ref[...]) + dot(fl, dh_ref[...]) + dot(fh, dl_ref[...]))
    for t in range(4):
        a = outs[0][:, t * 128:(t + 1) * 128]
        b = outs[1][:, t * 128:(t + 1) * 128]
        out_ref[2 * t] = jnp.where(lane < 64, a, pltpu.roll(b, 64, 1)).astype(BF)
        out_ref[2 * t + 1] = jnp.where(lane < 64, pltpu.roll(a, 64, 1), b).astype(BF)


def volume_call(rv, cells):
    cos, sin = dft_np()
    full = np.zeros((2, 256, 8, 2, 32))
    full[0, :, :, 0, :] = cos.reshape(256, 8, 32)
    full[1, :, :, 0, :] = -sin.reshape(256, 8, 32)
    full[0, :, :, 1, :] = sin.reshape(256, 8, 32)
    full[1, :, :, 1, :] = cos.reshape(256, 8, 32)
    dh, dl = split_np(full.reshape(512, 512))
    return pl.pallas_call(
        volume_kernel,
        out_shape=jax.ShapeDtypeStruct((8, 256, 128), BF),
        scratch_shapes=[pltpu.VMEM((1024, 256), F32)],
        compiler_params=pltpu.CompilerParams(vmem_limit_bytes=VMEM_LIMIT),
        name="volume_z",
    )(rv, cells, jnp.asarray(dh), jnp.asarray(dl))


def second_kernel(r1_ref, q_ref, dh_ref, dl_ref, out_ref):
    columns = []
    for xh in range(8):
        columns.append(jnp.concatenate([r1_ref[r, xh * 32:(xh + 1) * 32, :] for r in range(8)], axis=0))
    field = jnp.concatenate(columns, axis=1)
    turned = jnp.concatenate([dot(col, q_ref[...]).astype(BF) for col in columns], axis=1)
    both = jnp.concatenate([field, turned], axis=0)
    out = (dot(dh_ref[...], both) + dot(dl_ref[...], both)).astype(BF)
    for q in range(16):
        for xh in range(8):
            out_ref[q, xh] = out[q * 16:(q + 1) * 16, xh * 128:(xh + 1) * 128]


def second_call(r1):
    cos, sin = dft_np()
    dh, dl = split_np(np.concatenate([cos, sin], axis=1))
    turn = np.zeros((128, 128), np.float32)
    for g in range(2):
        for z in range(32):
            turn[g * 64 + 32 + z, g * 64 + z] = -1.0
            turn[g * 64 + z, g * 64 + 32 + z] = 1.0
    return pl.pallas_call(
        second_kernel,
        out_shape=jax.ShapeDtypeStruct((16, 8, 16, 128), BF),
        compiler_params=pltpu.CompilerParams(vmem_limit_bytes=VMEM_LIMIT),
        name="transform_y",
    )(r1, jnp.asarray(turn.astype(ml_dtypes.bfloat16)), jnp.asarray(dh), jnp.asarray(dl))


def third_kernel(r2_ref, dh_ref, dl_ref, out_ref, stage, lhs):
    stage[...] = r2_ref[...].astype(F32)
    for y in range(16):
        turned = jnp.transpose(stage[pl.ds(y, 128, stride=16), :])
        for g in range(4):
            lhs[g, pl.ds(y, 32, stride=16), :] = turned[g * 32:(g + 1) * 32, :]
    field = jnp.concatenate([lhs[g].astype(BF) for g in range(4)], axis=1)
    out = dot(field, dh_ref[...]) + dot(field, dl_ref[...])
    out_ref[0] = out[:, 0:256]
    out_ref[1] = out[:, 256:512]


def third_call(r2):
    cos, sin = dft_np()
    full = np.zeros((2, 2, 128, 2, 256))
    for xl in range(2):
        full[xl, 0, :, 0, :] = cos[xl::2]
        full[xl, 1, :, 0, :] = -sin[xl::2]
        full[xl, 0, :, 1, :] = sin[xl::2]
        full[xl, 1, :, 1, :] = cos[xl::2]
    dh, dl = split_np(full.reshape(512, 512))
    return pl.pallas_call(
        third_kernel,
        out_shape=jax.ShapeDtypeStruct((2, 512, 256), F32),
        scratch_shapes=[pltpu.VMEM((2048, 128), F32), pltpu.VMEM((4, 512, 128), F32)],
        compiler_params=pltpu.CompilerParams(vmem_limit_bytes=VMEM_LIMIT),
        name="transform_x",
    )(r2, jnp.asarray(dh), jnp.asarray(dl))


def by_rows(x):
    n = x.shape[0]
    return x.reshape(n, 2, 64, 128).transpose(0, 2, 1, 3).reshape(n, 128, 128)


def local(images, projections, noise_weight, shift_ids, owner_ids, cell_ids, weight_ids, interp_table):
    devices = lax.axis_size("img") * lax.axis_size("ori")
    n_ori = lax.axis_size("ori")
    n_slot = devices * CAP
    slots, send_cells = slots_call(owner_ids, cell_ids, n_slot)
    got_cells = lax.all_to_all(
        send_cells.reshape(devices, CAP), ("img", "ori"), split_axis=0, concat_axis=0, tiled=True)

    aligned, scores, stats = align_call(
        by_rows(images), by_rows(projections), noise_weight.reshape(64, 128), shift_ids)
    all_stats = lax.all_to_all(
        jnp.broadcast_to(stats[None], (n_ori,) + stats.shape), "ori", split_axis=0, concat_axis=0, tiled=True)
    partial, loglik = slices_call(scores, all_stats, aligned)
    loglik = loglik[:, :IB].reshape(-1)
    pieces = lax.all_to_all(partial, "img", split_axis=0, concat_axis=0, tiled=True)
    send = interp_call(pieces, weight_ids, slots, interp_table.reshape(-1, 128), n_slot)
    got = lax.all_to_all(
        send.reshape(devices, CAP, 256), ("img", "ori"), split_axis=0, concat_axis=0, tiled=True)
    first = volume_call(got.reshape(n_slot, 256), got_cells.reshape(1, n_slot))
    second = second_call(lax.all_to_all(first, "img", split_axis=0, concat_axis=0, tiled=True))
    third = lax.all_to_all(second, "ori", split_axis=0, concat_axis=0, tiled=True)
    realspace = third_call(third.reshape(2048, 128))
    return realspace.reshape(2, 32, 16, 256), loglik


def solution(mesh):
    placed = (
        P("img", None, None),
        P("ori", None, None),
        P(),
        P("img", None),
        P("ori", "img"),
        P("ori", "img"),
        P("ori", "img"),
        P(),
    )
    return jax.shard_map(
        local,
        mesh=mesh,
        in_specs=placed,
        out_specs=(P(None, "img", "ori", None), P("img")),
        check_vma=False,
    )
```

```python
import math

import jax
import jax.numpy as jnp
import ml_dtypes
import numpy as np
from jax import lax
from jax.experimental import pallas as pl
from jax.experimental.pallas import tpu as pltpu
from jax.sharding import PartitionSpec as P

BF = jnp.bfloat16
F32 = jnp.float32
I32 = jnp.int32

IB = 64
PITCH = IB + 8
GR = 16
NA = 5
CAP = 24
VMEM_LIMIT = 56 * 1024 * 1024


def split_np(a):
    high = a.astype(ml_dtypes.bfloat16)
    low = (a - high.astype(np.float64)).astype(ml_dtypes.bfloat16)
    return high, low


def dft_np():
    k = np.arange(256)
    ang = 2.0 * math.pi * ((k[:, None] * k[None, :]) % 256) / 256.0
    return np.cos(ang) / 16.0, np.sin(ang) / 16.0


def dot(a, b):
    return lax.dot_general(a, b, (((1,), (0,)), ((), ())), preferred_element_type=F32)


def split(a):
    high = a.astype(BF)
    return high, (a - high.astype(F32)).astype(BF)


def align_kernel(x_ref, pr_ref, nw_ref, sh_ref, ex_ref, aa_ref, ab_ref, sc_ref, st_ref,
                 xf, wk, pn, ph, stp, even, odd):
    b = pl.program_id(0)

    def rows_of(r):
        return pl.ds(pl.multiple_of(r * PITCH, 8), IB)

    @pl.when(b == 0)
    def _():
        def chunk(oc, carry):
            for i in range(IB):
                xf[pl.ds(i, 128, stride=PITCH), :] = pr_ref[oc * IB + i].astype(F32)
            rows = pl.ds(pl.multiple_of(oc * IB, IB), IB)

            def ky_step(ky, acc):
                noise = nw_ref[pl.ds(ky, 1), :]
                for p in range(2):
                    v = xf[rows_of(2 * ky + p), :]
                    vn = v * noise
                    wk[rows, pl.ds(pl.multiple_of(ky * 256 + p * 128, 128), 128)] = vn.astype(BF)
                    acc = acc + v * vn
                return acc
            acc = lax.fori_loop(0, 64, ky_step, jnp.zeros((IB, 128), F32), unroll=4)
            pn[rows, :] = jnp.broadcast_to(jnp.sum(acc, axis=1, keepdims=True) * 0.5, (IB, 128))
            return carry
        lax.fori_loop(0, 128 // IB, chunk, 0)

    for i in range(IB):
        xf[pl.ds(i, 128, stride=PITCH), :] = x_ref[i].astype(F32)

    for s in range(4):
        t = sh_ref[:, s:s + 1]
        ty = (t * 37) >> 8
        tx = t - ty * 7
        er = jnp.zeros((IB, 128), F32)
        ei = jnp.zeros((IB, 128), F32)
        sr = jnp.zeros((IB, 1), F32)
        si = jnp.zeros((IB, 1), F32)
        for d in range(7):
            hit = tx == d
            er = jnp.where(hit, ex_ref[d:d + 1, :], er)
            ei = jnp.where(hit, ex_ref[8 + d:9 + d, :], ei)
            ang = -2.0 * math.pi * (d - 3) / 128.0
            hity = ty == d
            sr = jnp.where(hity, math.cos(ang), sr)
            si = jnp.where(hity, math.sin(ang), si)
        ph[0, s] = er
        ph[1, s] = ei
        stp[0, s] = jnp.broadcast_to(sr, (IB, 128))
        stp[1, s] = jnp.broadcast_to(si, (IB, 128))

    def align_chunk(kc, buf):
        for s in range(4):
            for g in range(IB // GR):
                rows = slice(g * GR, (g + 1) * GR)
                pr = ph[0, s, rows]
                pi = ph[1, s, rows]
                sr = stp[0, s, rows]
                si = stp[1, s, rows]
                out = slice(s * IB + g * GR, s * IB + (g + 1) * GR)
                for j in range(8):
                    ky = kc * 8 + j
                    re = xf[pl.ds(pl.multiple_of(2 * ky * PITCH + g * GR, 8), GR), :]
                    im = xf[pl.ds(pl.multiple_of((2 * ky + 1) * PITCH + g * GR, 8), GR), :]
                    to, at = (aa_ref, kc * NA + j) if j < NA else (ab_ref, kc * (8 - NA) + j - NA)
                    lane = pl.multiple_of(at * 256, 256)
                    new_re = (re * pr - im * pi).astype(BF)
                    new_im = (re * pi + im * pr).astype(BF)
                    to[out, pl.ds(lane, 128)] = new_re
                    to[out, pl.ds(lane + 128, 128)] = new_im
                    buf[out, j * 256:j * 256 + 128] = new_re
                    buf[out, j * 256 + 128:j * 256 + 256] = new_im
                    pr, pi = pr * sr - pi * si, pr * si + pi * sr
                ph[0, s, rows] = pr
                ph[1, s, rows] = pi

    def score_chunk(kc, buf):
        lanes = pl.ds(pl.multiple_of(kc * 2048, 2048), 2048)
        return lax.dot_general(wk[:, lanes], buf[...], (((1,), (1,)), ((), ())),
                               preferred_element_type=F32)

    odd[...] = jnp.zeros_like(odd)

    def two_chunks(m, acc):
        acc = acc + score_chunk(jnp.maximum(2 * m - 1, 0), odd)
        align_chunk(2 * m, even)
        acc = acc + score_chunk(2 * m, even)
        align_chunk(2 * m + 1, odd)
        return acc
    acc = lax.fori_loop(0, 4, two_chunks, jnp.zeros((128, 4 * IB), F32))
    acc = acc + score_chunk(7, odd)
    sc = acc - pn[:, 0:1]
    sc_ref[0] = sc
    mx = jnp.max(sc, axis=0, keepdims=True)
    if IB == 64:
        mx = jnp.maximum(mx[:, 0:128], mx[:, 128:256])
    mx = jnp.maximum(mx, pltpu.roll(mx, 64, 1))
    if IB == 32:
        mx = jnp.maximum(mx, pltpu.roll(mx, 32, 1))
    wide = jnp.concatenate([mx] * (IB // 32), axis=1)
    tot = jnp.sum(jnp.exp(sc - wide), axis=0, keepdims=True)
    if IB == 64:
        tot = tot[:, 0:128] + tot[:, 128:256]
    tot = tot + pltpu.roll(tot, 64, 1)
    if IB == 32:
        tot = tot + pltpu.roll(tot, 32, 1)
    st_ref[0, pl.ds(b, 1), :] = mx
    st_ref[1, pl.ds(b, 1), :] = tot


def align_call(xv, pv, noise, shifts):
    n_img = xv.shape[0]
    steps = n_img // IB
    kx = np.arange(128) - 64
    ex = np.zeros((16, 128), np.float32)
    for d in range(7):
        ang = -2.0 * math.pi * ((kx * (d - 3)) % 128) / 128.0
        ex[d] = np.cos(ang)
        ex[8 + d] = np.sin(ang)
    whole3 = lambda b: (0, 0, 0)
    whole2 = lambda b: (0, 0)
    return pl.pallas_call(
        align_kernel,
        grid=(steps,),
        in_specs=[
            pl.BlockSpec((IB, 128, 128), lambda b: (b, 0, 0)),
            pl.BlockSpec((128, 128, 128), whole3, pipeline_mode=pl.Buffered(1)),
            pl.BlockSpec((64, 128), whole2),
            pl.BlockSpec((IB, 4), lambda b: (b, 0)),
            pl.BlockSpec((16, 128), whole2),
        ],
        out_specs=[
            pl.BlockSpec((4 * IB, 2048 * NA), lambda b: (b, 0)),
            pl.BlockSpec((4 * IB, 2048 * (8 - NA)), lambda b: (b, 0)),
            pl.BlockSpec((1, 128, 4 * IB), lambda b: (b, 0, 0)),
            pl.BlockSpec((2, steps, 128), whole3),
        ],
        out_shape=[
            jax.ShapeDtypeStruct((4 * n_img, 2048 * NA), BF),
            jax.ShapeDtypeStruct((4 * n_img, 2048 * (8 - NA)), BF),
            jax.ShapeDtypeStruct((steps, 128, 4 * IB), F32),
            jax.ShapeDtypeStruct((2, steps, 128), F32),
        ],
        scratch_shapes=[
            pltpu.VMEM((128 * PITCH, 128), F32),
            pltpu.VMEM((128, 16384), BF),
            pltpu.VMEM((128, 128), F32),
            pltpu.VMEM((2, 4, IB, 128), F32),
            pltpu.VMEM((2, 4, IB, 128), F32),
            pltpu.VMEM((4 * IB, 2048), BF),
            pltpu.VMEM((4 * IB, 2048), BF),
        ],
        compiler_params=pltpu.CompilerParams(vmem_limit_bytes=VMEM_LIMIT),
        name="align_scores",
    )(xv, pv, noise, shifts, jnp.asarray(ex))


def prob_of(sc_ref, st_ref, ll_ref, pt):
    n = st_ref.shape[0]
    peak = st_ref[0, 0]
    for q in range(1, n):
        peak = jnp.maximum(peak, st_ref[q, 0])
    total = jnp.zeros_like(peak)
    for q in range(n):
        total = total + st_ref[q, 1] * jnp.exp(st_ref[q, 0] - peak)
    ll_ref[...] = peak + jnp.log(total)
    inv = 1.0 / total
    for blk in range(sc_ref.shape[0]):
        wide_peak = jnp.concatenate([peak[blk:blk + 1, :]] * (IB // 32), axis=1)
        wide_inv = jnp.concatenate([inv[blk:blk + 1, :]] * (IB // 32), axis=1)
        pr = jnp.exp(sc_ref[blk] - wide_peak) * wide_inv
        pt[:, blk * 4 * IB:(blk + 1) * 4 * IB] = pr.astype(BF)


def store_blocks(out_ref, at, res):
    for c in range(res.shape[1] // 256):
        piece = res[:, c * 256:(c + 1) * 256].astype(BF)
        if at is None:
            out_ref[c] = piece
        else:
            out_ref[at, c] = piece


def first_slices_kernel(dest_ref, sc_ref, st_ref, a_ref, o0_ref, o1_ref, pt_ref, ll_ref):
    g = pl.program_id(0)

    @pl.when(g == 0)
    def _():
        prob_of(sc_ref, st_ref, ll_ref, pt_ref)
    res = dot(pt_ref[...], a_ref[...])

    @pl.when(g == 0)
    def _():
        store_blocks(o0_ref, None, res)

    @pl.when(g == 1)
    def _():
        store_blocks(o1_ref, None, res)


def first_slices(dests, sc, st, a):
    rows = a.shape[0]
    steps = sc.shape[0]
    piece = jax.ShapeDtypeStruct((NA, 128, 256), BF)
    keep3 = lambda g, d: (0, 0, 0)
    return pl.pallas_call(
        first_slices_kernel,
        grid_spec=pltpu.PrefetchScalarGridSpec(
            num_scalar_prefetch=1,
            grid=(2,),
            in_specs=[
                pl.BlockSpec(sc.shape, keep3),
                pl.BlockSpec(st.shape, lambda g, d: (0, 0, 0, 0)),
                pl.BlockSpec((rows, 256 * NA), lambda g, d: (0, d[g])),
            ],
            out_specs=[
                pl.BlockSpec(piece.shape, keep3),
                pl.BlockSpec(piece.shape, keep3),
                pl.BlockSpec((128, rows), lambda g, d: (0, 0)),
                pl.BlockSpec((steps, 128), lambda g, d: (0, 0)),
            ],
        ),
        out_shape=[
            piece, piece,
            jax.ShapeDtypeStruct((128, rows), BF),
            jax.ShapeDtypeStruct((steps, 128), F32),
        ],
        compiler_params=pltpu.CompilerParams(vmem_limit_bytes=VMEM_LIMIT),
        name="first_slices",
    )(dests, sc, st, a)


def more_slices(dests, pt, a, width, n_out, name):
    n = dests.shape[0]
    rows = a.shape[0]
    blocks = width // 256

    def kernel(dest_ref, pt_ref, a_ref, *outs):
        g = pl.program_id(0)
        res = dot(pt_ref[...], a_ref[...])
        if n_out == 1:
            store_blocks(outs[0], 0, res)
            return
        for k in range(n):
            @pl.when(g == k)
            def _():
                store_blocks(outs[k], None, res)

    if n_out == 1:
        shapes = [jax.ShapeDtypeStruct((n, blocks, 128, 256), BF)]
        specs = [pl.BlockSpec((1, blocks, 128, 256), lambda g, d: (g, 0, 0, 0))]
    else:
        shapes = [jax.ShapeDtypeStruct((blocks, 128, 256), BF)] * n
        specs = [pl.BlockSpec((blocks, 128, 256), lambda g, d: (0, 0, 0))] * n
    return pl.pallas_call(
        kernel,
        grid_spec=pltpu.PrefetchScalarGridSpec(
            num_scalar_prefetch=1,
            grid=(n,),
            in_specs=[
                pl.BlockSpec((128, rows), lambda g, d: (0, 0)),
                pl.BlockSpec((rows, width), lambda g, d: (0, d[g])),
            ],
            out_specs=specs,
        ),
        out_shape=shapes,
        compiler_params=pltpu.CompilerParams(vmem_limit_bytes=VMEM_LIMIT),
        name=name,
    )(dests, pt, a)


def added(*pieces):
    total = pieces[0].astype(F32)
    for piece in pieces[1:]:
        total = total + piece.astype(F32)
    return total.astype(BF)


def reduce_slices(sc, st, aa, ab):
    n_img = lax.axis_size("img")
    n_y = n_img // 2
    me = lax.axis_index("img")
    my_y = me >> 1
    my_z = me & 1

    def dest(dy, dz):
        return ((my_y + dy) & (n_y - 1)) * 2 + ((my_z + dz) & 1)

    def table(pairs):
        return jnp.stack([dest(*pair) for pair in pairs]).astype(I32)

    def shift_y(x, d):
        perm = [(y * 2 + z, ((y + d) % n_y) * 2 + z) for y in range(n_y) for z in range(2)]
        return lax.ppermute(x, "img", perm)

    def swap_z(x):
        return lax.ppermute(x, "img", [(i, i ^ 1) for i in range(n_img)])

    a20, a21, pt, loglik = first_slices(table([(2, 0), (2, 1)]), sc, st, aa)
    u = shift_y(a20, 1)
    v = shift_y(a21, -1)
    bz, = more_slices(table([(2, 1), (1, 1), (3, 1), (0, 1)]), pt, ab, 256 * (8 - NA), 1, "slices_z")
    bz = swap_z(bz)
    a10, a11, a30, a31 = more_slices(
        table([(1, 0), (1, 1), (3, 0), (3, 1)]), pt, aa, 256 * NA, 4, "slices_y")
    from_left1 = shift_y(a11, 1)
    from_right0 = shift_y(a30, -1)
    a00, a01 = more_slices(table([(0, 0), (0, 1)]), pt, aa, 256 * NA, 2, "slices_own")
    b0, = more_slices(table([(2, 0), (1, 0), (3, 0), (0, 0)]), pt, ab, 256 * (8 - NA), 1, "slices_b")
    from_left0 = shift_y(added(a10, u), 1)
    from_right1 = shift_y(added(a31, v), -1)
    tb = added(b0, bz)
    ub = shift_y(tb[0][:, :64], 1)
    vb = shift_y(tb[0][:, 64:], -1)
    other = swap_z(added(a01, from_left1, from_right1))
    left_b = shift_y(added(tb[1], jnp.pad(ub, ((0, 0), (0, 64), (0, 0)))), 1)
    right_b = shift_y(added(tb[2], jnp.pad(vb, ((0, 0), (64, 0), (0, 0)))), -1)
    return (a00, from_left0, from_right0, other), (tb[3], left_b, right_b), loglik


def slots_kernel(ow_ref, ce_ref, slot_ref, cell_ref):
    lane = lax.broadcasted_iota(I32, (128, 128), 1)
    sub = lax.broadcasted_iota(I32, (128, 128), 0)
    lower = (sub >= lane).astype(F32).astype(BF)
    base = jnp.zeros((1, 128), F32)
    slot_all = jnp.zeros((128, 128), F32)
    cell_all = jnp.zeros((128, 128), F32)
    columns = []
    for c in range(8):
        oc = ow_ref[:, c:c + 1]
        hit = (oc == lane).astype(F32)
        run = dot(lower, hit.astype(BF)) + base
        rank = jnp.sum(run * hit, axis=1, keepdims=True) - 1.0
        base = base + jnp.sum(hit, axis=0, keepdims=True)
        slot = oc.astype(F32) * float(CAP) + rank
        columns.append(slot.astype(I32))
        slot_all = jnp.where(lane == c, slot, slot_all)
        cell_all = jnp.where(lane == c, ce_ref[:, c:c + 1].astype(F32), cell_all)
    slot_ref[...] = jnp.transpose(slot_all)[0:8, :].astype(I32)
    cells_t = jnp.transpose(cell_all)[0:8, :]
    high = jnp.floor(cells_t * (1.0 / 32.0))
    low = cells_t - high * 32.0
    row = lax.broadcasted_iota(I32, (16, 128), 0)
    n_slot = cell_ref.shape[1]
    slot_lane = lax.broadcasted_iota(I32, (128, n_slot), 1)
    acc = jnp.zeros((16, n_slot), F32)
    for c in range(8):
        parts = jnp.where(row == 0, high[c:c + 1, :],
                          jnp.where(row == 1, low[c:c + 1, :], jnp.where(row == 2, 1.0, 0.0)))
        pick = (columns[c] == slot_lane).astype(F32).astype(BF)
        acc = acc + dot(parts.astype(BF), pick)
    cell = acc[0:1, :] * 32.0 + acc[1:2, :]
    cell_ref[...] = jnp.where(acc[2:3, :] > 0.5, cell, -1.0).astype(I32)


def slots_call(owners, cells, n_slot):
    return pl.pallas_call(
        slots_kernel,
        out_shape=[jax.ShapeDtypeStruct((8, 128), I32), jax.ShapeDtypeStruct((1, n_slot), I32)],
        compiler_params=pltpu.CompilerParams(vmem_limit_bytes=VMEM_LIMIT),
        name="slots",
    )(owners, cells)


WSTEP = 4


def interpolate(parts, c0, wid_ref, tab_ref, blk, tid, acc):
    n = parts[0].shape[0]
    for c in range(n):
        tid[c * 128:(c + 1) * 128, :] = jnp.broadcast_to(wid_ref[:, c0 + c:c0 + c + 1], (128, 128))
        total = parts[0][c].astype(F32)
        for part in parts[1:]:
            total = total + part[c].astype(F32)
        total = total.astype(BF).astype(F32)
        for p in range(2):
            blk[(p * n + c) * 128:(p * n + c + 1) * 128, :] = total[:, p * 128:(p + 1) * 128]
    acc[...] = jnp.zeros_like(acc)

    def step(g, carry):
        table = tab_ref[pl.ds(pl.multiple_of(g * (WSTEP * 128), WSTEP * 128), WSTEP * 128), :]
        for k in range(2 * n):
            rows = slice(k * 128, (k + 1) * 128)
            c = k % n
            values = blk[rows, :]
            ids = tid[c * 128:(c + 1) * 128, :]
            lhs = jnp.concatenate(
                [jnp.where(ids == g * WSTEP + u, values, 0.0).astype(BF) for u in range(WSTEP)], axis=1)
            acc[rows, :] += dot(lhs, table)
        return carry
    lax.fori_loop(0, 64 // WSTEP, step, 0)


def interp_a_kernel(p0, p1, p2, p3, wid_ref, tab_ref, out_ref, blk, tid, acc):
    interpolate([p0, p1, p2, p3], 0, wid_ref, tab_ref, blk, tid, acc)
    n = p0.shape[0] * 128
    out_ref[:, 0:128] = acc[0:n, :].astype(BF)
    out_ref[:, 128:256] = acc[n:2 * n, :].astype(BF)


def interp_b_kernel(p0, p1, p2, con_ref, wid_ref, slot_ref, tab_ref, out_ref, blk, tid, acc, con):
    interpolate([p0, p1, p2], NA, wid_ref, tab_ref, blk, tid, acc)
    n = p0.shape[0] * 128
    con[0:NA * 128, :] = con_ref[...]
    con[NA * 128:, 0:128] = acc[0:n, :].astype(BF)
    con[NA * 128:, 128:256] = acc[n:2 * n, :].astype(BF)

    def place(k, carry):
        row = lax.broadcasted_iota(I32, (384, 128), 0) + k * 384
        pick = jnp.concatenate(
            [jnp.where(slot_ref[c:c + 1, :] == row, 1.0, 0.0).astype(BF) for c in range(8)], axis=1)
        out_ref[pl.ds(pl.multiple_of(k * 384, 384), 384), :] = dot(pick, con[...]).astype(BF)
        return carry
    lax.fori_loop(0, out_ref.shape[0] // 384, place, 0)


def interp_scratch(n):
    return [
        pltpu.VMEM((2 * n * 128, 128), F32),
        pltpu.VMEM((n * 128, 128), I32),
        pltpu.VMEM((2 * n * 128, 128), F32),
    ]


def interp_call(parts_a, parts_b, wid, slots, table, n_slot):
    con = pl.pallas_call(
        interp_a_kernel,
        out_shape=jax.ShapeDtypeStruct((NA * 128, 256), BF),
        scratch_shapes=interp_scratch(NA),
        compiler_params=pltpu.CompilerParams(vmem_limit_bytes=VMEM_LIMIT),
        name="interpolate_a",
    )(*parts_a, wid, table)
    return pl.pallas_call(
        interp_b_kernel,
        out_shape=jax.ShapeDtypeStruct((n_slot, 256), BF),
        scratch_shapes=interp_scratch(8 - NA) + [pltpu.VMEM((1024, 256), BF)],
        compiler_params=pltpu.CompilerParams(vmem_limit_bytes=VMEM_LIMIT),
        name="interpolate_b",
    )(*parts_b, con, wid, slots, table)


def volume_kernel(rv_ref, cell_ref, dh_ref, dl_ref, out_ref, vol):
    n_slot = rv_ref.shape[0]
    cell = cell_ref[...]
    half = cell & 1
    y = (cell >> 1) & 31
    x = cell >> 6
    where = half * 512 + (x & 1) * 256 + (x >> 1) * 32 + y
    where = jnp.where(cell < 0, -1, where)

    def land(k, carry):
        row = lax.broadcasted_iota(I32, (128, n_slot), 0) + k * 128
        pick = jnp.where(where == row, 1.0, 0.0).astype(BF)
        vol[pl.ds(pl.multiple_of(k * 128, 128), 128), :] = dot(pick, rv_ref[...])
        return carry
    lax.fori_loop(0, 8, land, 0)
    lane = lax.broadcasted_iota(I32, (256, 128), 1)
    outs = []
    for xl in range(2):
        lo = slice(xl * 256, (xl + 1) * 256)
        hi = slice(512 + xl * 256, 512 + (xl + 1) * 256)
        field = jnp.concatenate(
            [vol[lo, 0:128], vol[hi, 0:128], vol[lo, 128:256], vol[hi, 128:256]], axis=1)
        fh, fl = split(field)
        outs.append(dot(fh, dh_ref[...]) + dot(fl, dh_ref[...]) + dot(fh, dl_ref[...]))
    for t in range(4):
        a = outs[0][:, t * 128:(t + 1) * 128]
        b = outs[1][:, t * 128:(t + 1) * 128]
        out_ref[2 * t] = jnp.where(lane < 64, a, pltpu.roll(b, 64, 1)).astype(BF)
        out_ref[2 * t + 1] = jnp.where(lane < 64, pltpu.roll(a, 64, 1), b).astype(BF)


def volume_call(rv, cells):
    cos, sin = dft_np()
    full = np.zeros((2, 256, 8, 2, 32))
    full[0, :, :, 0, :] = cos.reshape(256, 8, 32)
    full[1, :, :, 0, :] = -sin.reshape(256, 8, 32)
    full[0, :, :, 1, :] = sin.reshape(256, 8, 32)
    full[1, :, :, 1, :] = cos.reshape(256, 8, 32)
    dh, dl = split_np(full.reshape(512, 512))
    return pl.pallas_call(
        volume_kernel,
        out_shape=jax.ShapeDtypeStruct((8, 256, 128), BF),
        scratch_shapes=[pltpu.VMEM((1024, 256), F32)],
        compiler_params=pltpu.CompilerParams(vmem_limit_bytes=VMEM_LIMIT),
        name="volume_z",
    )(rv, cells, jnp.asarray(dh), jnp.asarray(dl))


def second_kernel(r1_ref, q_ref, dh_ref, dl_ref, out_ref):
    columns = []
    for xh in range(8):
        columns.append(jnp.concatenate([r1_ref[r, xh * 32:(xh + 1) * 32, :] for r in range(8)], axis=0))
    field = jnp.concatenate(columns, axis=1)
    turned = jnp.concatenate([dot(col, q_ref[...]).astype(BF) for col in columns], axis=1)
    both = jnp.concatenate([field, turned], axis=0)
    out = (dot(dh_ref[...], both) + dot(dl_ref[...], both)).astype(BF)
    for q in range(16):
        for xh in range(8):
            out_ref[q, xh] = out[q * 16:(q + 1) * 16, xh * 128:(xh + 1) * 128]


def second_call(r1):
    cos, sin = dft_np()
    dh, dl = split_np(np.concatenate([cos, sin], axis=1))
    turn = np.zeros((128, 128), np.float32)
    for g in range(2):
        for z in range(32):
            turn[g * 64 + 32 + z, g * 64 + z] = -1.0
            turn[g * 64 + z, g * 64 + 32 + z] = 1.0
    return pl.pallas_call(
        second_kernel,
        out_shape=jax.ShapeDtypeStruct((16, 8, 16, 128), BF),
        compiler_params=pltpu.CompilerParams(vmem_limit_bytes=VMEM_LIMIT),
        name="transform_y",
    )(r1, jnp.asarray(turn.astype(ml_dtypes.bfloat16)), jnp.asarray(dh), jnp.asarray(dl))


def third_kernel(r2_ref, dh_ref, dl_ref, out_ref, stage, lhs):
    stage[...] = r2_ref[...].astype(F32)
    for y in range(16):
        turned = jnp.transpose(stage[pl.ds(y, 128, stride=16), :])
        for g in range(4):
            lhs[g, pl.ds(y, 32, stride=16), :] = turned[g * 32:(g + 1) * 32, :]
    field = jnp.concatenate([lhs[g].astype(BF) for g in range(4)], axis=1)
    out = dot(field, dh_ref[...]) + dot(field, dl_ref[...])
    out_ref[0] = out[:, 0:256]
    out_ref[1] = out[:, 256:512]


def third_call(r2):
    cos, sin = dft_np()
    full = np.zeros((2, 2, 128, 2, 256))
    for xl in range(2):
        full[xl, 0, :, 0, :] = cos[xl::2]
        full[xl, 1, :, 0, :] = -sin[xl::2]
        full[xl, 0, :, 1, :] = sin[xl::2]
        full[xl, 1, :, 1, :] = cos[xl::2]
    dh, dl = split_np(full.reshape(512, 512))
    return pl.pallas_call(
        third_kernel,
        out_shape=jax.ShapeDtypeStruct((2, 512, 256), F32),
        scratch_shapes=[pltpu.VMEM((2048, 128), F32), pltpu.VMEM((4, 512, 128), F32)],
        compiler_params=pltpu.CompilerParams(vmem_limit_bytes=VMEM_LIMIT),
        name="transform_x",
    )(r2, jnp.asarray(dh), jnp.asarray(dl))


def by_rows(x):
    n = x.shape[0]
    return x.reshape(n, 2, 64, 128).transpose(0, 2, 1, 3).reshape(n, 128, 128)


def local(images, projections, noise_weight, shift_ids, owner_ids, cell_ids, weight_ids, interp_table):
    devices = lax.axis_size("img") * lax.axis_size("ori")
    n_ori = lax.axis_size("ori")
    n_slot = devices * CAP
    slots, send_cells = slots_call(owner_ids, cell_ids, n_slot)
    got_cells = lax.all_to_all(
        send_cells.reshape(devices, CAP), ("img", "ori"), split_axis=0, concat_axis=0, tiled=True)

    aa, ab, scores, stats = align_call(
        by_rows(images), by_rows(projections), noise_weight.reshape(64, 128), shift_ids)
    all_stats = lax.all_to_all(
        jnp.broadcast_to(stats[None], (n_ori,) + stats.shape), "ori", split_axis=0, concat_axis=0, tiled=True)
    parts_a, parts_b, loglik = reduce_slices(scores, all_stats, aa, ab)
    loglik = loglik[:, :IB].reshape(-1)
    send = interp_call(parts_a, parts_b, weight_ids, slots, interp_table.reshape(-1, 128), n_slot)
    got = lax.all_to_all(
        send.reshape(devices, CAP, 256), ("img", "ori"), split_axis=0, concat_axis=0, tiled=True)
    first = volume_call(got.reshape(n_slot, 256), got_cells.reshape(1, n_slot))
    second = second_call(lax.all_to_all(first, "img", split_axis=0, concat_axis=0, tiled=True))
    third = lax.all_to_all(second, "ori", split_axis=0, concat_axis=0, tiled=True)
    realspace = third_call(third.reshape(2048, 128))
    return realspace.reshape(2, 32, 16, 256), loglik


def solution(mesh):
    placed = (
        P("img", None, None),
        P("ori", None, None),
        P(),
        P("img", None),
        P("ori", "img"),
        P("ori", "img"),
        P("ori", "img"),
        P(),
    )
    return jax.shard_map(
        local,
        mesh=mesh,
        in_specs=placed,
        out_specs=(P(None, "img", "ori", None), P("img")),
        check_vma=False,
    )
```

```python
import math

import jax
import jax.numpy as jnp
import ml_dtypes
import numpy as np
from jax import lax
from jax.experimental import pallas as pl
from jax.experimental.pallas import tpu as pltpu
from jax.sharding import PartitionSpec as P

BF = jnp.bfloat16
F32 = jnp.float32
I32 = jnp.int32

IB = 64
PITCH = IB + 8
GR = 16
NA = 4
CAP = 24
VMEM_LIMIT = 56 * 1024 * 1024


def split_np(a):
    high = a.astype(ml_dtypes.bfloat16)
    low = (a - high.astype(np.float64)).astype(ml_dtypes.bfloat16)
    return high, low


def dft_np():
    k = np.arange(256)
    ang = 2.0 * math.pi * ((k[:, None] * k[None, :]) % 256) / 256.0
    return np.cos(ang) / 16.0, np.sin(ang) / 16.0


def dot(a, b):
    return lax.dot_general(a, b, (((1,), (0,)), ((), ())), preferred_element_type=F32)


def split(a):
    high = a.astype(BF)
    return high, (a - high.astype(F32)).astype(BF)


def align_kernel(x_ref, pr_ref, nw_ref, sh_ref, ex_ref, a_ref, sc_ref, st_ref,
                 xf, wk, pn, ph, stp, even, odd):
    b = pl.program_id(0)

    def rows_of(r):
        return pl.ds(pl.multiple_of(r * PITCH, 8), IB)

    @pl.when(b == 0)
    def _():
        def chunk(oc, carry):
            for i in range(IB):
                xf[pl.ds(i, 128, stride=PITCH), :] = pr_ref[oc * IB + i].astype(F32)
            rows = pl.ds(pl.multiple_of(oc * IB, IB), IB)

            def ky_step(ky, acc):
                noise = nw_ref[pl.ds(ky, 1), :]
                for p in range(2):
                    v = xf[rows_of(2 * ky + p), :]
                    vn = v * noise
                    wk[rows, pl.ds(pl.multiple_of(ky * 256 + p * 128, 128), 128)] = vn.astype(BF)
                    acc = acc + v * vn
                return acc
            acc = lax.fori_loop(0, 64, ky_step, jnp.zeros((IB, 128), F32), unroll=4)
            pn[rows, :] = jnp.broadcast_to(jnp.sum(acc, axis=1, keepdims=True) * 0.5, (IB, 128))
            return carry
        lax.fori_loop(0, 128 // IB, chunk, 0)

    for i in range(IB):
        xf[pl.ds(i, 128, stride=PITCH), :] = x_ref[i].astype(F32)

    for s in range(4):
        t = sh_ref[:, s:s + 1]
        ty = (t * 37) >> 8
        tx = t - ty * 7
        er = jnp.zeros((IB, 128), F32)
        ei = jnp.zeros((IB, 128), F32)
        sr = jnp.zeros((IB, 1), F32)
        si = jnp.zeros((IB, 1), F32)
        for d in range(7):
            hit = tx == d
            er = jnp.where(hit, ex_ref[d:d + 1, :], er)
            ei = jnp.where(hit, ex_ref[8 + d:9 + d, :], ei)
            ang = -2.0 * math.pi * (d - 3) / 128.0
            hity = ty == d
            sr = jnp.where(hity, math.cos(ang), sr)
            si = jnp.where(hity, math.sin(ang), si)
        ph[0, s] = er
        ph[1, s] = ei
        stp[0, s] = jnp.broadcast_to(sr, (IB, 128))
        stp[1, s] = jnp.broadcast_to(si, (IB, 128))

    def align_chunk(kc, buf):
        for s in range(4):
            for g in range(IB // GR):
                rows = slice(g * GR, (g + 1) * GR)
                pr = ph[0, s, rows]
                pi = ph[1, s, rows]
                sr = stp[0, s, rows]
                si = stp[1, s, rows]
                out = slice(s * IB + g * GR, s * IB + (g + 1) * GR)
                for j in range(8):
                    ky = kc * 8 + j
                    re = xf[pl.ds(pl.multiple_of(2 * ky * PITCH + g * GR, 8), GR), :]
                    im = xf[pl.ds(pl.multiple_of((2 * ky + 1) * PITCH + g * GR, 8), GR), :]
                    lane = pl.multiple_of(ky * 256, 256)
                    new_re = (re * pr - im * pi).astype(BF)
                    new_im = (re * pi + im * pr).astype(BF)
                    a_ref[out, pl.ds(lane, 128)] = new_re
                    a_ref[out, pl.ds(lane + 128, 128)] = new_im
                    buf[out, j * 256:j * 256 + 128] = new_re
                    buf[out, j * 256 + 128:j * 256 + 256] = new_im
                    pr, pi = pr * sr - pi * si, pr * si + pi * sr
                ph[0, s, rows] = pr
                ph[1, s, rows] = pi

    def score_chunk(kc, buf):
        lanes = pl.ds(pl.multiple_of(kc * 2048, 2048), 2048)
        return lax.dot_general(buf[...], wk[:, lanes], (((1,), (1,)), ((), ())),
                               preferred_element_type=F32)

    odd[...] = jnp.zeros_like(odd)

    def two_chunks(m, acc):
        acc = acc + score_chunk(jnp.maximum(2 * m - 1, 0), odd)
        align_chunk(2 * m, even)
        acc = acc + score_chunk(2 * m, even)
        align_chunk(2 * m + 1, odd)
        return acc
    acc = lax.fori_loop(0, 4, two_chunks, jnp.zeros((4 * IB, 128), F32))
    acc = acc + score_chunk(7, odd)
    sc = jnp.transpose(acc) - pn[:, 0:1]
    sc_ref[0] = sc
    mx = jnp.max(sc, axis=0, keepdims=True)
    if IB == 64:
        mx = jnp.maximum(mx[:, 0:128], mx[:, 128:256])
    mx = jnp.maximum(mx, pltpu.roll(mx, 64, 1))
    if IB == 32:
        mx = jnp.maximum(mx, pltpu.roll(mx, 32, 1))
    wide = jnp.concatenate([mx] * (IB // 32), axis=1)
    tot = jnp.sum(jnp.exp(sc - wide), axis=0, keepdims=True)
    if IB == 64:
        tot = tot[:, 0:128] + tot[:, 128:256]
    tot = tot + pltpu.roll(tot, 64, 1)
    if IB == 32:
        tot = tot + pltpu.roll(tot, 32, 1)
    for q in range(st_ref.shape[0]):
        st_ref[q, 0, pl.ds(b, 1), :] = mx
        st_ref[q, 1, pl.ds(b, 1), :] = tot


def align_call(xv, pv, noise, shifts, n_ori=16):
    n_img = xv.shape[0]
    steps = n_img // IB
    kx = np.arange(128) - 64
    ex = np.zeros((16, 128), np.float32)
    for d in range(7):
        ang = -2.0 * math.pi * ((kx * (d - 3)) % 128) / 128.0
        ex[d] = np.cos(ang)
        ex[8 + d] = np.sin(ang)
    whole3 = lambda b: (0, 0, 0)
    whole2 = lambda b: (0, 0)
    return pl.pallas_call(
        align_kernel,
        grid=(steps,),
        in_specs=[
            pl.BlockSpec((IB, 128, 128), lambda b: (b, 0, 0)),
            pl.BlockSpec((128, 128, 128), whole3, pipeline_mode=pl.Buffered(1)),
            pl.BlockSpec((64, 128), whole2),
            pl.BlockSpec((IB, 4), lambda b: (b, 0)),
            pl.BlockSpec((16, 128), whole2),
        ],
        out_specs=[
            pl.BlockSpec((4 * IB, 16384), lambda b: (b, 0)),
            pl.BlockSpec((1, 128, 4 * IB), lambda b: (b, 0, 0)),
            pl.BlockSpec((n_ori, 2, steps, 128), lambda b: (0, 0, 0, 0)),
        ],
        out_shape=[
            jax.ShapeDtypeStruct((4 * n_img, 16384), BF),
            jax.ShapeDtypeStruct((steps, 128, 4 * IB), F32),
            jax.ShapeDtypeStruct((n_ori, 2, steps, 128), F32),
        ],
        scratch_shapes=[
            pltpu.VMEM((128 * PITCH, 128), F32),
            pltpu.VMEM((128, 16384), BF),
            pltpu.VMEM((128, 128), F32),
            pltpu.VMEM((2, 4, IB, 128), F32),
            pltpu.VMEM((2, 4, IB, 128), F32),
            pltpu.VMEM((4 * IB, 2048), BF),
            pltpu.VMEM((4 * IB, 2048), BF),
        ],
        compiler_params=pltpu.CompilerParams(vmem_limit_bytes=VMEM_LIMIT),
        name="align_scores",
    )(xv, pv, noise, shifts, jnp.asarray(ex))


def prob_of(sc_ref, st_ref, ll_ref, pt):
    n = st_ref.shape[0]
    peak = st_ref[0, 0]
    for q in range(1, n):
        peak = jnp.maximum(peak, st_ref[q, 0])
    total = jnp.zeros_like(peak)
    for q in range(n):
        total = total + st_ref[q, 1] * jnp.exp(st_ref[q, 0] - peak)
    ll_ref[...] = peak + jnp.log(total)
    inv = 1.0 / total
    for blk in range(sc_ref.shape[0]):
        wide_peak = jnp.concatenate([peak[blk:blk + 1, :]] * (IB // 32), axis=1)
        wide_inv = jnp.concatenate([inv[blk:blk + 1, :]] * (IB // 32), axis=1)
        pr = jnp.exp(sc_ref[blk] - wide_peak) * wide_inv
        pt[:, blk * 4 * IB:(blk + 1) * 4 * IB] = pr.astype(BF)


def slices_call(dests, a, sizes, name, pt=None, sc=None, st=None):
    rows = a.shape[0]
    first = pt is None
    places = []
    for k, size in enumerate(sizes):
        places += [(k, None if size == 1 else m) for m in range(size)]

    def kernel(dest_ref, *refs):
        g = pl.program_id(0)
        if first:
            sc_ref, st_ref, a_ref = refs[:3]
            outs = refs[3:]
            pt_ref, ll_ref = outs[len(sizes):]

            @pl.when(g == 0)
            def _():
                prob_of(sc_ref, st_ref, ll_ref, pt_ref)
        else:
            pt_ref, a_ref = refs[:2]
            outs = refs[2:]
        res = dot(pt_ref[...], a_ref[...])
        for step, (k, m) in enumerate(places):
            @pl.when(g == step)
            def _():
                for c in range(NA):
                    piece = res[:, c * 256:(c + 1) * 256].astype(BF)
                    if m is None:
                        outs[k][c] = piece
                    else:
                        outs[k][m, c] = piece

    def keep(shape):
        return pl.BlockSpec(shape, lambda g, d: (0,) * len(shape))

    shapes = [(NA, 128, 256) if size == 1 else (size, NA, 128, 256) for size in sizes]
    out_shape = [jax.ShapeDtypeStruct(shape, BF) for shape in shapes]
    if first:
        inputs = [sc, st]
        out_shape += [jax.ShapeDtypeStruct((128, rows), BF), jax.ShapeDtypeStruct((sc.shape[0], 128), F32)]
    else:
        inputs = [pt]
    return pl.pallas_call(
        kernel,
        grid_spec=pltpu.PrefetchScalarGridSpec(
            num_scalar_prefetch=1,
            grid=(len(places),),
            in_specs=[keep(x.shape) for x in inputs]
            + [pl.BlockSpec((rows, 256 * NA), lambda g, d: (0, d[g]))],
            out_specs=[keep(x.shape) for x in out_shape],
        ),
        out_shape=out_shape,
        compiler_params=pltpu.CompilerParams(vmem_limit_bytes=VMEM_LIMIT),
        name=name,
    )(dests, *inputs, a)


def added(*pieces):
    total = pieces[0].astype(F32)
    for piece in pieces[1:]:
        total = total + piece.astype(F32)
    return total.astype(BF)


def after(x, y):
    return lax.optimization_barrier((x, y))[0]


def reduce_slices(sc, st, a):
    n_img = lax.axis_size("img")
    n_y = n_img // 2
    me = lax.axis_index("img")
    my_y = me >> 1
    my_z = me & 1

    def table(groups):
        return jnp.stack([
            (((my_y + dy) & (n_y - 1)) * 2 + ((my_z + dz) & 1)) * 2 + part for part, dy, dz in groups]).astype(I32)

    def shift_y(x, d):
        perm = [(y * 2 + z, ((y + d) % n_y) * 2 + z) for y in range(n_y) for z in range(2)]
        return lax.ppermute(x, "img", perm)

    def swap_z(x):
        return lax.ppermute(x, "img", [(i, i ^ 1) for i in range(n_img)])

    a20, a21, pt, loglik = slices_call(
        table([(0, 2, 0), (0, 2, 1)]), a, (1, 1), "slices_first", sc=sc, st=st)
    u = shift_y(a20, 1)
    v = shift_y(a21, -1)
    bz2, bzr = slices_call(
        table([(1, 2, 1), (1, 1, 1), (1, 3, 1), (1, 0, 1)]), a, (1, 3), "slices_z", pt=pt)
    pt = after(pt, bz2)
    bz2 = swap_z(bz2)
    bzr = swap_z(bzr)
    a10, a11, a30, a31 = slices_call(
        table([(0, 1, 0), (0, 1, 1), (0, 3, 0), (0, 3, 1)]), a, (1, 1, 1, 1), "slices_y", pt=pt)
    pt = after(pt, a11)
    from_left1 = shift_y(a11, 1)
    from_right0 = shift_y(a30, -1)
    from_left0 = shift_y(added(a10, u), 1)
    from_right1 = shift_y(added(a31, v), -1)
    b02, b01, b03, b00, a00, a01 = slices_call(
        table([(1, 2, 0), (1, 1, 0), (1, 3, 0), (1, 0, 0), (0, 0, 0), (0, 0, 1)]), a, (1,) * 6, "slices_own", pt=pt)
    ub = shift_y(added(b02[:, :64], bz2[:, :64]), 1)
    vb = shift_y(added(b02[:, 64:], bz2[:, 64:]), -1)
    other = swap_z(added(a01, from_left1, from_right1))
    left_b = shift_y(added(b01, bzr[0], jnp.pad(ub, ((0, 0), (0, 64), (0, 0)))), 1)
    right_b = shift_y(added(b03, bzr[1], jnp.pad(vb, ((0, 0), (64, 0), (0, 0)))), -1)
    return (a00, from_left0, from_right0, other), (b00, bzr, left_b, right_b), loglik, b00


def slots_kernel(ow_ref, ce_ref, slot_ref, cell_ref):
    lane = lax.broadcasted_iota(I32, (128, 128), 1)
    sub = lax.broadcasted_iota(I32, (128, 128), 0)
    lower = (sub >= lane).astype(F32).astype(BF)
    base = jnp.zeros((1, 128), F32)
    slot_all = jnp.zeros((128, 128), F32)
    cell_all = jnp.zeros((128, 128), F32)
    columns = []
    for c in range(8):
        oc = ow_ref[:, c:c + 1]
        hit = (oc == lane).astype(F32)
        run = dot(lower, hit.astype(BF)) + base
        rank = jnp.sum(run * hit, axis=1, keepdims=True) - 1.0
        base = base + jnp.sum(hit, axis=0, keepdims=True)
        slot = oc.astype(F32) * float(CAP) + rank
        columns.append(slot.astype(I32))
        slot_all = jnp.where(lane == c, slot, slot_all)
        cell_all = jnp.where(lane == c, ce_ref[:, c:c + 1].astype(F32), cell_all)
    slot_ref[...] = jnp.transpose(slot_all)[0:8, :].astype(I32)
    cells_t = jnp.transpose(cell_all)[0:8, :]
    high = jnp.floor(cells_t * (1.0 / 32.0))
    low = cells_t - high * 32.0
    row = lax.broadcasted_iota(I32, (16, 128), 0)
    n_slot = cell_ref.shape[1]
    slot_lane = lax.broadcasted_iota(I32, (128, n_slot), 1)
    acc = jnp.zeros((16, n_slot), F32)
    for c in range(8):
        parts = jnp.where(row == 0, high[c:c + 1, :],
                          jnp.where(row == 1, low[c:c + 1, :], jnp.where(row == 2, 1.0, 0.0)))
        pick = (columns[c] == slot_lane).astype(F32).astype(BF)
        acc = acc + dot(parts.astype(BF), pick)
    cell = acc[0:1, :] * 32.0 + acc[1:2, :]
    cell_ref[...] = jnp.where(acc[2:3, :] > 0.5, cell, -1.0).astype(I32)


def slots_call(owners, cells, n_slot):
    return pl.pallas_call(
        slots_kernel,
        out_shape=[jax.ShapeDtypeStruct((8, 128), I32), jax.ShapeDtypeStruct((1, n_slot), I32)],
        compiler_params=pltpu.CompilerParams(vmem_limit_bytes=VMEM_LIMIT),
        name="slots",
    )(owners, cells)


WSTEP = 4


def interpolate(parts, c0, wid_ref, tab_ref, blk, tid, acc):
    n = parts[0].shape[0]
    for c in range(n):
        tid[c * 128:(c + 1) * 128, :] = jnp.broadcast_to(wid_ref[:, c0 + c:c0 + c + 1], (128, 128))
        total = jnp.zeros((128, 256), F32)
        for part in parts:
            total = total + (part[c] if len(part.shape) == 3 else part[part.shape[0] - 1, c]).astype(F32)
        total = total.astype(BF).astype(F32)
        for p in range(2):
            blk[(p * n + c) * 128:(p * n + c + 1) * 128, :] = total[:, p * 128:(p + 1) * 128]
    acc[...] = jnp.zeros_like(acc)

    def step(g, carry):
        table = tab_ref[pl.ds(pl.multiple_of(g * (WSTEP * 128), WSTEP * 128), WSTEP * 128), :]
        for k in range(2 * n):
            rows = slice(k * 128, (k + 1) * 128)
            c = k % n
            values = blk[rows, :]
            ids = tid[c * 128:(c + 1) * 128, :]
            lhs = jnp.concatenate(
                [jnp.where(ids == g * WSTEP + u, values, 0.0).astype(BF) for u in range(WSTEP)], axis=1)
            acc[rows, :] += dot(lhs, table)
        return carry
    lax.fori_loop(0, 64 // WSTEP, step, 0)


def interp_a_kernel(p0, p1, p2, p3, wid_ref, tab_ref, out_ref, blk, tid, acc):
    interpolate([p0, p1, p2, p3], 0, wid_ref, tab_ref, blk, tid, acc)
    n = p0.shape[0] * 128
    out_ref[:, 0:128] = acc[0:n, :].astype(BF)
    out_ref[:, 128:256] = acc[n:2 * n, :].astype(BF)


def interp_b_kernel(p0, p1, p2, p3, con_ref, wid_ref, slot_ref, tab_ref, out_ref, blk, tid, acc, con):
    interpolate([p0, p1, p2, p3], NA, wid_ref, tab_ref, blk, tid, acc)
    n = p0.shape[0] * 128
    con[0:NA * 128, :] = con_ref[...]
    con[NA * 128:, 0:128] = acc[0:n, :].astype(BF)
    con[NA * 128:, 128:256] = acc[n:2 * n, :].astype(BF)

    def place(k, carry):
        row = lax.broadcasted_iota(I32, (384, 128), 0) + k * 384
        pick = jnp.concatenate(
            [jnp.where(slot_ref[c:c + 1, :] == row, 1.0, 0.0).astype(BF) for c in range(8)], axis=1)
        out_ref[pl.ds(pl.multiple_of(k * 384, 384), 384), :] = dot(pick, con[...]).astype(BF)
        return carry
    lax.fori_loop(0, out_ref.shape[0] // 384, place, 0)


def interp_scratch(n):
    return [
        pltpu.VMEM((2 * n * 128, 128), F32),
        pltpu.VMEM((n * 128, 128), I32),
        pltpu.VMEM((2 * n * 128, 128), F32),
    ]


def interp_call(parts_a, parts_b, wid, slots, table, n_slot):
    con = pl.pallas_call(
        interp_a_kernel,
        out_shape=jax.ShapeDtypeStruct((NA * 128, 256), BF),
        scratch_shapes=interp_scratch(NA),
        compiler_params=pltpu.CompilerParams(vmem_limit_bytes=VMEM_LIMIT),
        name="interpolate_a",
    )(*parts_a, wid, table)
    return pl.pallas_call(
        interp_b_kernel,
        out_shape=jax.ShapeDtypeStruct((n_slot, 256), BF),
        scratch_shapes=interp_scratch(8 - NA) + [pltpu.VMEM((1024, 256), BF)],
        compiler_params=pltpu.CompilerParams(vmem_limit_bytes=VMEM_LIMIT),
        name="interpolate_b",
    )(*parts_b, con, wid, slots, table)


def volume_kernel(rv_ref, cell_ref, dh_ref, dl_ref, out_ref, vol):
    n_slot = rv_ref.shape[0]
    cell = cell_ref[...]
    half = cell & 1
    y = (cell >> 1) & 31
    x = cell >> 6
    where = half * 512 + (x & 1) * 256 + (x >> 1) * 32 + y
    where = jnp.where(cell < 0, -1, where)

    def land(k, carry):
        row = lax.broadcasted_iota(I32, (128, n_slot), 0) + k * 128
        pick = jnp.where(where == row, 1.0, 0.0).astype(BF)
        vol[pl.ds(pl.multiple_of(k * 128, 128), 128), :] = dot(pick, rv_ref[...])
        return carry
    lax.fori_loop(0, 8, land, 0)
    lane = lax.broadcasted_iota(I32, (256, 128), 1)
    outs = []
    for xl in range(2):
        lo = slice(xl * 256, (xl + 1) * 256)
        hi = slice(512 + xl * 256, 512 + (xl + 1) * 256)
        field = jnp.concatenate(
            [vol[lo, 0:128], vol[hi, 0:128], vol[lo, 128:256], vol[hi, 128:256]], axis=1)
        fh, fl = split(field)
        outs.append(dot(fh, dh_ref[...]) + dot(fl, dh_ref[...]) + dot(fh, dl_ref[...]))
    for t in range(4):
        a = outs[0][:, t * 128:(t + 1) * 128]
        b = outs[1][:, t * 128:(t + 1) * 128]
        out_ref[2 * t] = jnp.where(lane < 64, a, pltpu.roll(b, 64, 1)).astype(BF)
        out_ref[2 * t + 1] = jnp.where(lane < 64, pltpu.roll(a, 64, 1), b).astype(BF)


def volume_call(rv, cells):
    cos, sin = dft_np()
    full = np.zeros((2, 256, 8, 2, 32))
    full[0, :, :, 0, :] = cos.reshape(256, 8, 32)
    full[1, :, :, 0, :] = -sin.reshape(256, 8, 32)
    full[0, :, :, 1, :] = sin.reshape(256, 8, 32)
    full[1, :, :, 1, :] = cos.reshape(256, 8, 32)
    dh, dl = split_np(full.reshape(512, 512))
    return pl.pallas_call(
        volume_kernel,
        out_shape=jax.ShapeDtypeStruct((8, 256, 128), BF),
        scratch_shapes=[pltpu.VMEM((1024, 256), F32)],
        compiler_params=pltpu.CompilerParams(vmem_limit_bytes=VMEM_LIMIT),
        name="volume_z",
    )(rv, cells, jnp.asarray(dh), jnp.asarray(dl))


def second_kernel(r1_ref, q_ref, dh_ref, dl_ref, out_ref):
    columns = []
    for xh in range(8):
        columns.append(jnp.concatenate([r1_ref[r, xh * 32:(xh + 1) * 32, :] for r in range(8)], axis=0))
    field = jnp.concatenate(columns, axis=1)
    turned = jnp.concatenate([dot(col, q_ref[...]).astype(BF) for col in columns], axis=1)
    both = jnp.concatenate([field, turned], axis=0)
    out = (dot(dh_ref[...], both) + dot(dl_ref[...], both)).astype(BF)
    for q in range(16):
        for xh in range(8):
            out_ref[q, xh] = out[q * 16:(q + 1) * 16, xh * 128:(xh + 1) * 128]


def second_call(r1):
    cos, sin = dft_np()
    dh, dl = split_np(np.concatenate([cos, sin], axis=1))
    turn = np.zeros((128, 128), np.float32)
    for g in range(2):
        for z in range(32):
            turn[g * 64 + 32 + z, g * 64 + z] = -1.0
            turn[g * 64 + z, g * 64 + 32 + z] = 1.0
    return pl.pallas_call(
        second_kernel,
        out_shape=jax.ShapeDtypeStruct((16, 8, 16, 128), BF),
        compiler_params=pltpu.CompilerParams(vmem_limit_bytes=VMEM_LIMIT),
        name="transform_y",
    )(r1, jnp.asarray(turn.astype(ml_dtypes.bfloat16)), jnp.asarray(dh), jnp.asarray(dl))


def third_kernel(r2_ref, dh_ref, dl_ref, out_ref, stage, lhs):
    stage[...] = r2_ref[...].astype(F32)
    for y in range(16):
        turned = jnp.transpose(stage[pl.ds(y, 128, stride=16), :])
        for g in range(4):
            lhs[g, pl.ds(y, 32, stride=16), :] = turned[g * 32:(g + 1) * 32, :]
    field = jnp.concatenate([lhs[g].astype(BF) for g in range(4)], axis=1)
    out = dot(field, dh_ref[...]) + dot(field, dl_ref[...])
    out_ref[0] = out[:, 0:256]
    out_ref[1] = out[:, 256:512]


def third_call(r2):
    cos, sin = dft_np()
    full = np.zeros((2, 2, 128, 2, 256))
    for xl in range(2):
        full[xl, 0, :, 0, :] = cos[xl::2]
        full[xl, 1, :, 0, :] = -sin[xl::2]
        full[xl, 0, :, 1, :] = sin[xl::2]
        full[xl, 1, :, 1, :] = cos[xl::2]
    dh, dl = split_np(full.reshape(512, 512))
    return pl.pallas_call(
        third_kernel,
        out_shape=jax.ShapeDtypeStruct((2, 512, 256), F32),
        scratch_shapes=[pltpu.VMEM((2048, 128), F32), pltpu.VMEM((4, 512, 128), F32)],
        compiler_params=pltpu.CompilerParams(vmem_limit_bytes=VMEM_LIMIT),
        name="transform_x",
    )(r2, jnp.asarray(dh), jnp.asarray(dl))


def by_rows(x):
    n = x.shape[0]
    return x.reshape(n, 2, 64, 128).transpose(0, 2, 1, 3).reshape(n, 128, 128)


def local(images, projections, noise_weight, shift_ids, owner_ids, cell_ids, weight_ids, interp_table):
    devices = lax.axis_size("img") * lax.axis_size("ori")
    n_ori = lax.axis_size("ori")
    n_slot = devices * CAP
    a, scores, stats = align_call(
        by_rows(images), by_rows(projections), noise_weight.reshape(64, 128), shift_ids, n_ori)
    all_stats = lax.all_to_all(stats, "ori", split_axis=0, concat_axis=0, tiled=True)
    parts_a, parts_b, loglik, last = reduce_slices(scores, all_stats, a)
    loglik = loglik[:, :IB].reshape(-1)
    slots, send_cells = slots_call(after(owner_ids, last), cell_ids, n_slot)
    got_cells = lax.all_to_all(
        send_cells.reshape(devices, CAP), ("img", "ori"), split_axis=0, concat_axis=0, tiled=True)
    send = interp_call(parts_a, parts_b, weight_ids, slots, interp_table.reshape(-1, 128), n_slot)
    got = lax.all_to_all(
        send.reshape(devices, CAP, 256), ("img", "ori"), split_axis=0, concat_axis=0, tiled=True)
    first = volume_call(got.reshape(n_slot, 256), got_cells.reshape(1, n_slot))
    second = second_call(lax.all_to_all(first, "img", split_axis=0, concat_axis=0, tiled=True))
    third = lax.all_to_all(second, "ori", split_axis=0, concat_axis=0, tiled=True)
    realspace = third_call(third.reshape(2048, 128))
    return realspace.reshape(2, 32, 16, 256), loglik


def solution(mesh):
    placed = (
        P("img", None, None),
        P("ori", None, None),
        P(),
        P("img", None),
        P("ori", "img"),
        P("ori", "img"),
        P("ori", "img"),
        P(),
    )
    return jax.shard_map(
        local,
        mesh=mesh,
        in_specs=placed,
        out_specs=(P(None, "img", "ori", None), P("img")),
        check_vma=False,
    )
```

```python
import math
from functools import partial

import jax
import jax.numpy as jnp
import ml_dtypes
import numpy as np
from jax import lax
from jax.experimental import pallas as pl
from jax.experimental.pallas import tpu as pltpu
from jax.sharding import PartitionSpec as P

BF = jnp.bfloat16
F32 = jnp.float32
I32 = jnp.int32

IB = 64
PITCH = IB + 8
GR = 16
NA = 4
CAP = 24
VMEM_LIMIT = 56 * 1024 * 1024


def split_np(a):
    high = a.astype(ml_dtypes.bfloat16)
    low = (a - high.astype(np.float64)).astype(ml_dtypes.bfloat16)
    return high, low


def dft_np():
    k = np.arange(256)
    ang = 2.0 * math.pi * ((k[:, None] * k[None, :]) % 256) / 256.0
    return np.cos(ang) / 16.0, np.sin(ang) / 16.0


def dot(a, b):
    return lax.dot_general(a, b, (((1,), (0,)), ((), ())), preferred_element_type=F32)


def split(a):
    high = a.astype(BF)
    return high, (a - high.astype(F32)).astype(BF)


def align_kernel(x_ref, pr_ref, nw_ref, sh_ref, ex_ref, a_ref, sc_ref, st_ref,
                 xf, wk, pn, ph, stp, even, odd):
    b = pl.program_id(0)

    def rows_of(r):
        return pl.ds(pl.multiple_of(r * PITCH, 8), IB)

    @pl.when(b == 0)
    def _():
        def chunk(oc, carry):
            for i in range(IB):
                xf[pl.ds(i, 128, stride=PITCH), :] = pr_ref[oc * IB + i].astype(F32)
            rows = pl.ds(pl.multiple_of(oc * IB, IB), IB)

            def ky_step(ky, acc):
                noise = nw_ref[pl.ds(ky, 1), :]
                for p in range(2):
                    v = xf[rows_of(2 * ky + p), :]
                    vn = v * noise
                    wk[rows, pl.ds(pl.multiple_of(ky * 256 + p * 128, 128), 128)] = vn.astype(BF)
                    acc = acc + v * vn
                return acc
            acc = lax.fori_loop(0, 64, ky_step, jnp.zeros((IB, 128), F32), unroll=4)
            pn[rows, :] = jnp.broadcast_to(jnp.sum(acc, axis=1, keepdims=True) * 0.5, (IB, 128))
            return carry
        lax.fori_loop(0, 128 // IB, chunk, 0)

    for i in range(IB):
        xf[pl.ds(i, 128, stride=PITCH), :] = x_ref[i].astype(F32)

    for s in range(4):
        t = sh_ref[:, s:s + 1]
        ty = (t * 37) >> 8
        tx = t - ty * 7
        er = jnp.zeros((IB, 128), F32)
        ei = jnp.zeros((IB, 128), F32)
        sr = jnp.zeros((IB, 1), F32)
        si = jnp.zeros((IB, 1), F32)
        for d in range(7):
            hit = tx == d
            er = jnp.where(hit, ex_ref[d:d + 1, :], er)
            ei = jnp.where(hit, ex_ref[8 + d:9 + d, :], ei)
            ang = -2.0 * math.pi * (d - 3) / 128.0
            hity = ty == d
            sr = jnp.where(hity, math.cos(ang), sr)
            si = jnp.where(hity, math.sin(ang), si)
        ph[0, s] = er
        ph[1, s] = ei
        stp[0, s] = jnp.broadcast_to(sr, (IB, 128))
        stp[1, s] = jnp.broadcast_to(si, (IB, 128))

    def align_chunk(kc, buf):
        for s in range(4):
            for g in range(IB // GR):
                rows = slice(g * GR, (g + 1) * GR)
                pr = ph[0, s, rows]
                pi = ph[1, s, rows]
                sr = stp[0, s, rows]
                si = stp[1, s, rows]
                out = slice(s * IB + g * GR, s * IB + (g + 1) * GR)
                for j in range(8):
                    ky = kc * 8 + j
                    re = xf[pl.ds(pl.multiple_of(2 * ky * PITCH + g * GR, 8), GR), :]
                    im = xf[pl.ds(pl.multiple_of((2 * ky + 1) * PITCH + g * GR, 8), GR), :]
                    lane = pl.multiple_of(ky * 256, 256)
                    new_re = (re * pr - im * pi).astype(BF)
                    new_im = (re * pi + im * pr).astype(BF)
                    a_ref[out, pl.ds(lane, 128)] = new_re
                    a_ref[out, pl.ds(lane + 128, 128)] = new_im
                    buf[out, j * 256:j * 256 + 128] = new_re
                    buf[out, j * 256 + 128:j * 256 + 256] = new_im
                    pr, pi = pr * sr - pi * si, pr * si + pi * sr
                ph[0, s, rows] = pr
                ph[1, s, rows] = pi

    def score_chunk(kc, buf):
        lanes = pl.ds(pl.multiple_of(kc * 2048, 2048), 2048)
        return lax.dot_general(buf[...], wk[:, lanes], (((1,), (1,)), ((), ())),
                               preferred_element_type=F32)

    odd[...] = jnp.zeros_like(odd)

    def two_chunks(m, acc):
        acc = acc + score_chunk(jnp.maximum(2 * m - 1, 0), odd)
        align_chunk(2 * m, even)
        acc = acc + score_chunk(2 * m, even)
        align_chunk(2 * m + 1, odd)
        return acc
    acc = lax.fori_loop(0, 4, two_chunks, jnp.zeros((4 * IB, 128), F32))
    acc = acc + score_chunk(7, odd)
    sc = jnp.transpose(acc) - pn[:, 0:1]
    sc_ref[0] = sc
    mx = jnp.max(sc, axis=0, keepdims=True)
    if IB == 64:
        mx = jnp.maximum(mx[:, 0:128], mx[:, 128:256])
    mx = jnp.maximum(mx, pltpu.roll(mx, 64, 1))
    if IB == 32:
        mx = jnp.maximum(mx, pltpu.roll(mx, 32, 1))
    wide = jnp.concatenate([mx] * (IB // 32), axis=1)
    tot = jnp.sum(jnp.exp(sc - wide), axis=0, keepdims=True)
    if IB == 64:
        tot = tot[:, 0:128] + tot[:, 128:256]
    tot = tot + pltpu.roll(tot, 64, 1)
    if IB == 32:
        tot = tot + pltpu.roll(tot, 32, 1)
    for q in range(st_ref.shape[0]):
        st_ref[q, 0, pl.ds(b, 1), :] = mx
        st_ref[q, 1, pl.ds(b, 1), :] = tot


def align_call(xv, pv, noise, shifts, n_ori=16):
    n_img = xv.shape[0]
    steps = n_img // IB
    kx = np.arange(128) - 64
    ex = np.zeros((16, 128), np.float32)
    for d in range(7):
        ang = -2.0 * math.pi * ((kx * (d - 3)) % 128) / 128.0
        ex[d] = np.cos(ang)
        ex[8 + d] = np.sin(ang)
    whole3 = lambda b: (0, 0, 0)
    whole2 = lambda b: (0, 0)
    return pl.pallas_call(
        align_kernel,
        grid=(steps,),
        in_specs=[
            pl.BlockSpec((IB, 128, 128), lambda b: (b, 0, 0)),
            pl.BlockSpec((128, 128, 128), whole3, pipeline_mode=pl.Buffered(1)),
            pl.BlockSpec((64, 128), whole2),
            pl.BlockSpec((IB, 4), lambda b: (b, 0)),
            pl.BlockSpec((16, 128), whole2),
        ],
        out_specs=[
            pl.BlockSpec((4 * IB, 16384), lambda b: (b, 0)),
            pl.BlockSpec((1, 128, 4 * IB), lambda b: (b, 0, 0)),
            pl.BlockSpec((n_ori, 2, steps, 128), lambda b: (0, 0, 0, 0)),
        ],
        out_shape=[
            jax.ShapeDtypeStruct((4 * n_img, 16384), BF),
            jax.ShapeDtypeStruct((steps, 128, 4 * IB), F32),
            jax.ShapeDtypeStruct((n_ori, 2, steps, 128), F32),
        ],
        scratch_shapes=[
            pltpu.VMEM((128 * PITCH, 128), F32),
            pltpu.VMEM((128, 16384), BF),
            pltpu.VMEM((128, 128), F32),
            pltpu.VMEM((2, 4, IB, 128), F32),
            pltpu.VMEM((2, 4, IB, 128), F32),
            pltpu.VMEM((4 * IB, 2048), BF),
            pltpu.VMEM((4 * IB, 2048), BF),
        ],
        compiler_params=pltpu.CompilerParams(vmem_limit_bytes=VMEM_LIMIT),
        name="align_scores",
    )(xv, pv, noise, shifts, jnp.asarray(ex))


def prob_of(sc_ref, st_ref, ll_ref, pt):
    n = st_ref.shape[0]
    peak = st_ref[0, 0]
    for q in range(1, n):
        peak = jnp.maximum(peak, st_ref[q, 0])
    total = jnp.zeros_like(peak)
    for q in range(n):
        total = total + st_ref[q, 1] * jnp.exp(st_ref[q, 0] - peak)
    ll_ref[...] = peak + jnp.log(total)
    inv = 1.0 / total
    for blk in range(sc_ref.shape[0]):
        wide_peak = jnp.concatenate([peak[blk:blk + 1, :]] * (IB // 32), axis=1)
        wide_inv = jnp.concatenate([inv[blk:blk + 1, :]] * (IB // 32), axis=1)
        pr = jnp.exp(sc_ref[blk] - wide_peak) * wide_inv
        pt[:, blk * 4 * IB:(blk + 1) * 4 * IB] = pr.astype(BF)


def slices_call(dests, a, sizes, name, pt=None, sc=None, st=None):
    rows = a.shape[0]
    width = 256 * NA
    first = pt is None
    places = []
    for k, size in enumerate(sizes):
        places += [(k, None if size == 1 else m) for m in range(size)]
    n = len(places)

    def kernel(dest_ref, *refs):
        inputs = refs[:-2]
        buf, sem = refs[-2:]
        if first:
            sc_ref, st_ref, a_ref = inputs[:3]
            outs = inputs[3:]
            pt_ref, ll_ref = outs[len(sizes):]
        else:
            pt_ref, a_ref = inputs[:2]
            outs = inputs[2:]

        def copy(step):
            lanes = pl.ds(pl.multiple_of(dest_ref[step] * width, width), width)
            return pltpu.make_async_copy(a_ref.at[:, lanes], buf.at[step], sem.at[step])

        for step in range(n):
            copy(step).start()
        if first:
            prob_of(sc_ref, st_ref, ll_ref, pt_ref)
        for step, (k, m) in enumerate(places):
            copy(step).wait()
            res = dot(pt_ref[...], buf[step])
            for c in range(NA):
                piece = res[:, c * 256:(c + 1) * 256].astype(BF)
                if m is None:
                    outs[k][c] = piece
                else:
                    outs[k][m, c] = piece

    def keep(shape):
        return pl.BlockSpec(shape, lambda g, d: (0,) * len(shape))

    shapes = [(NA, 128, 256) if size == 1 else (size, NA, 128, 256) for size in sizes]
    out_shape = [jax.ShapeDtypeStruct(shape, BF) for shape in shapes]
    if first:
        inputs = [sc, st]
        out_shape += [jax.ShapeDtypeStruct((128, rows), BF), jax.ShapeDtypeStruct((sc.shape[0], 128), F32)]
    else:
        inputs = [pt]
    return pl.pallas_call(
        kernel,
        grid_spec=pltpu.PrefetchScalarGridSpec(
            num_scalar_prefetch=1,
            grid=(1,),
            in_specs=[keep(x.shape) for x in inputs] + [pl.BlockSpec(memory_space=pl.ANY)],
            out_specs=[keep(x.shape) for x in out_shape],
            scratch_shapes=[pltpu.VMEM((n, rows, width), BF), pltpu.SemaphoreType.DMA((n,))],
        ),
        out_shape=out_shape,
        compiler_params=pltpu.CompilerParams(vmem_limit_bytes=VMEM_LIMIT),
        name=name,
    )(dests, *inputs, a)


def added(*pieces):
    total = pieces[0].astype(F32)
    for piece in pieces[1:]:
        total = total + piece.astype(F32)
    return total.astype(BF)


def after(x, y):
    return lax.optimization_barrier((x, y))[0]


def reduce_slices(sc, st, a, plan):
    n_img = lax.axis_size("img")
    n_y = n_img // 2
    me = lax.axis_index("img")
    my_y = me >> 1
    my_z = me & 1

    def table(groups):
        return jnp.stack([
            (((my_y + dy) & (n_y - 1)) * 2 + ((my_z + dz) & 1)) * 2 + part for part, dy, dz in groups]).astype(I32)

    def shift_y(x, d):
        perm = [(y * 2 + z, ((y + d) % n_y) * 2 + z) for y in range(n_y) for z in range(2)]
        return lax.ppermute(x, "img", perm)

    def swap_z(x):
        return lax.ppermute(x, "img", [(i, i ^ 1) for i in range(n_img)])

    a20, a21, bz, pt, loglik = slices_call(
        table([(0, 2, 0), (0, 2, 1), (1, 2, 1), (1, 1, 1), (1, 3, 1), (1, 0, 1)]),
        a, (1, 1, 4), "slices_first", sc=sc, st=st)
    u = shift_y(a20, 1)
    v = shift_y(a21, -1)
    bz = swap_z(bz)
    to_left, to_right, b02, b01, b03, b00, a00, a01 = slices_call(
        table([(0, 1, 0), (0, 1, 1), (0, 3, 0), (0, 3, 1),
               (1, 2, 0), (1, 1, 0), (1, 3, 0), (1, 0, 0), (0, 0, 0), (0, 0, 1)]),
        a, (2, 2, 1, 1, 1, 1, 1, 1), "slices_rest", pt=pt)
    to_left = added(to_left, jnp.pad(u[None], ((0, 1), (0, 0), (0, 0), (0, 0))))
    to_right = added(to_right, jnp.pad(v[None], ((1, 0), (0, 0), (0, 0), (0, 0))))
    left = shift_y(to_left, 1)
    right = shift_y(to_right, -1)
    pos, slots, send_cells = plan(to_left, to_right)
    b02 = after(b02, pos)
    ub = shift_y(added(b02[:, :64], bz[0][:, :64]), 1)
    vb = shift_y(added(b02[:, 64:], bz[0][:, 64:]), -1)
    other = swap_z(added(a01, left[1], right[1]))
    left_b = shift_y(added(b01, bz[1], jnp.pad(ub, ((0, 0), (0, 64), (0, 0)))), 1)
    right_b = shift_y(added(b03, bz[2], jnp.pad(vb, ((0, 0), (64, 0), (0, 0)))), -1)
    return ((a00, left, right, other), (None, 0, 0, None)), ((b00, bz, left_b, right_b), (None, 3, None, None)), loglik, pos, slots, send_cells


def columns_of(rows8):
    return jnp.transpose(jnp.concatenate([rows8, jnp.zeros((120, 128), F32)], axis=0))


def two_parts(rows8, unit):
    high = jnp.floor(rows8 * (1.0 / unit))
    return high, rows8 - high * unit


def slots_kernel(ow_ref, ce_ref, wi_ref, pos_ref, slot_ref, cell_ref):
    lane = lax.broadcasted_iota(I32, (128, 128), 1)
    sub = lax.broadcasted_iota(I32, (128, 128), 0)
    lane_f = lane.astype(F32)
    lower = (sub >= lane).astype(F32).astype(BF)
    before = (sub < lane).astype(F32).astype(BF)
    owners = columns_of(ow_ref[...].astype(F32))
    weights = columns_of(wi_ref[...].astype(F32))
    base = jnp.zeros((1, 128), F32)
    base_w = jnp.zeros((1, 128), F32)
    slots = jnp.zeros((128, 128), F32)
    pos = jnp.zeros((128, 128), F32)
    slot_columns = []
    ranks = []
    for c in range(8):
        oc = owners[:, c:c + 1]
        hit = (oc == lane_f).astype(F32)
        run = dot(lower, hit.astype(BF)) + base
        rank = jnp.sum(run * hit, axis=1, keepdims=True) - 1.0
        base = base + jnp.sum(hit, axis=0, keepdims=True)
        slot = oc * float(CAP) + rank
        slot_columns.append(slot)
        slots = jnp.where(lane == c, slot, slots)
        hit = (weights[:, c:c + 1] == lane_f).astype(F32)
        run = dot(lower, hit.astype(BF)) + base_w
        ranks.append(jnp.sum(run * hit, axis=1, keepdims=True) - 1.0)
        base_w = base_w + jnp.sum(hit, axis=0, keepdims=True)
    high, low = two_parts(jnp.broadcast_to(base_w, (16, 128)), 32.0)
    start = (dot(high.astype(BF), before) * 32.0 + dot(low.astype(BF), before))[0:1, :]
    pos_columns = []
    for c in range(8):
        hit = weights[:, c:c + 1] == lane_f
        column = ranks[c] + jnp.sum(jnp.where(hit, start, 0.0), axis=1, keepdims=True)
        pos_columns.append(column)
        pos = jnp.where(lane == c, column, pos)
    pos_ref[...] = jnp.transpose(pos)[0:8, :].astype(I32)

    row = lax.broadcasted_iota(I32, (16, 128), 0)

    def scatter(parts_of, columns, n):
        to = lax.broadcasted_iota(I32, (128, n), 1).astype(F32)
        acc = jnp.zeros((16, n), F32)
        for c in range(8):
            high, low = parts_of(c)
            parts = jnp.where(row == 0, high, jnp.where(row == 1, low, jnp.where(row == 2, 1.0, 0.0)))
            acc = acc + dot(parts.astype(BF), (columns[c] == to).astype(F32).astype(BF))
        return acc

    slot_high, slot_low = two_parts(jnp.transpose(slots)[0:8, :], 64.0)
    acc = scatter(lambda c: (slot_high[c:c + 1, :], slot_low[c:c + 1, :]), pos_columns, 1024)
    slot_ref[...] = (acc[0:1, :] * 64.0 + acc[1:2, :]).astype(I32)
    cell_high, cell_low = two_parts(ce_ref[...].astype(F32), 32.0)
    acc = scatter(lambda c: (cell_high[c:c + 1, :], cell_low[c:c + 1, :]), slot_columns, cell_ref.shape[1])
    cell = acc[0:1, :] * 32.0 + acc[1:2, :]
    cell_ref[...] = jnp.where(acc[2:3, :] > 0.5, cell, -1.0).astype(I32)


def slots_call(owners, cells, weights, n_slot):
    return pl.pallas_call(
        slots_kernel,
        out_shape=[
            jax.ShapeDtypeStruct((8, 128), I32),
            jax.ShapeDtypeStruct((1, 1024), I32),
            jax.ShapeDtypeStruct((1, n_slot), I32),
        ],
        compiler_params=pltpu.CompilerParams(vmem_limit_bytes=VMEM_LIMIT),
        name="slots",
    )(owners, cells, weights)


WSTEP = 4
CHUNK = 128


def interp_kernel(picks, *refs):
    n_a, n_b = len(picks[0]), len(picks[1])
    parts = (refs[:n_a], refs[n_a:n_a + n_b])
    wi_ref, pos_ref, slot_ref, tab_ref, out_ref, raw, srt, con = refs[n_a + n_b:]
    weights = columns_of(wi_ref[...].astype(F32))
    for c in range(8):
        which, at = (0, c) if c < NA else (1, c - NA)
        total = jnp.zeros((128, 256), F32)
        for part, pick in zip(parts[which], picks[which]):
            total = total + (part[at] if pick is None else part[pick, at]).astype(F32)
        rows = slice(c * 128, (c + 1) * 128)
        raw[rows, 0:256] = total.astype(BF)
        raw[rows, 256:384] = jnp.broadcast_to(weights[:, c:c + 1], (128, 128)).astype(BF)

    def sort(k, carry):
        row = lax.broadcasted_iota(I32, (256, 128), 0) + k * 256
        pick = jnp.concatenate(
            [jnp.where(pos_ref[c:c + 1, :] == row, 1.0, 0.0).astype(BF) for c in range(8)], axis=1)
        srt[pl.ds(pl.multiple_of(k * 256, 256), 256), :] = dot(pick, raw[...]).astype(BF)
        return carry
    lax.fori_loop(0, 4, sort, 0)

    zero = jnp.zeros((CHUNK, 128), BF)

    def chunk(k, carry):
        rows = pl.ds(pl.multiple_of(k * CHUNK, CHUNK), CHUNK)
        ids = srt[rows, 256:384]
        ids_f = ids.astype(F32)
        lowest = jnp.min(ids_f[0:8, :]).astype(I32) >> 2
        highest = jnp.max(ids_f[CHUNK - 8:CHUNK, :]).astype(I32) >> 2

        def step(g, acc):
            pieces = []
            for p in range(2):
                values = srt[rows, p * 128:(p + 1) * 128]
                marks = [jnp.full((CHUNK, 128), (g * WSTEP + u).astype(F32), F32).astype(BF)
                         for u in range(WSTEP)]
                pieces.append(jnp.concatenate([jnp.where(ids == mark, values, zero) for mark in marks], axis=1))
            table = tab_ref[pl.ds(pl.multiple_of(g * (WSTEP * 128), WSTEP * 128), WSTEP * 128), :]
            return acc + dot(jnp.concatenate(pieces, axis=0), table)
        acc = lax.fori_loop(lowest, highest + 1, step, jnp.zeros((2 * CHUNK, 128), F32))
        con[rows, 0:128] = acc[0:CHUNK, :].astype(BF)
        con[rows, 128:256] = acc[CHUNK:, :].astype(BF)
        return carry
    lax.fori_loop(0, 1024 // CHUNK, chunk, 0)

    def place(k, carry):
        row = lax.broadcasted_iota(I32, (384, 1024), 0) + k * 384
        pick = jnp.where(slot_ref[...] == row, 1.0, 0.0).astype(BF)
        out_ref[pl.ds(pl.multiple_of(k * 384, 384), 384), :] = dot(pick, con[...]).astype(BF)
        return carry
    lax.fori_loop(0, out_ref.shape[0] // 384, place, 0)


def interp_call(parts_a, parts_b, weights, pos, slots, table, n_slot):
    return pl.pallas_call(
        partial(interp_kernel, (parts_a[1], parts_b[1])),
        out_shape=jax.ShapeDtypeStruct((n_slot, 256), BF),
        scratch_shapes=[
            pltpu.VMEM((1024, 384), BF),
            pltpu.VMEM((1024, 384), BF),
            pltpu.VMEM((1024, 256), BF),
        ],
        compiler_params=pltpu.CompilerParams(vmem_limit_bytes=VMEM_LIMIT),
        name="interpolate",
    )(*parts_a[0], *parts_b[0], weights, pos, slots, table)


def volume_kernel(rv_ref, cell_ref, dh_ref, dl_ref, out_ref, vol):
    n_slot = rv_ref.shape[0]
    cell = cell_ref[...]
    half = cell & 1
    y = (cell >> 1) & 31
    x = cell >> 6
    where = half * 512 + (x & 1) * 256 + (x >> 1) * 32 + y
    where = jnp.where(cell < 0, -1, where)

    def land(k, carry):
        row = lax.broadcasted_iota(I32, (128, n_slot), 0) + k * 128
        pick = jnp.where(where == row, 1.0, 0.0).astype(BF)
        vol[pl.ds(pl.multiple_of(k * 128, 128), 128), :] = dot(pick, rv_ref[...])
        return carry
    lax.fori_loop(0, 8, land, 0)
    lane = lax.broadcasted_iota(I32, (256, 128), 1)
    outs = []
    for xl in range(2):
        lo = slice(xl * 256, (xl + 1) * 256)
        hi = slice(512 + xl * 256, 512 + (xl + 1) * 256)
        field = jnp.concatenate(
            [vol[lo, 0:128], vol[hi, 0:128], vol[lo, 128:256], vol[hi, 128:256]], axis=1)
        fh, fl = split(field)
        outs.append(dot(fh, dh_ref[...]) + dot(fl, dh_ref[...]) + dot(fh, dl_ref[...]))
    for t in range(4):
        a = outs[0][:, t * 128:(t + 1) * 128]
        b = outs[1][:, t * 128:(t + 1) * 128]
        out_ref[2 * t] = jnp.where(lane < 64, a, pltpu.roll(b, 64, 1)).astype(BF)
        out_ref[2 * t + 1] = jnp.where(lane < 64, pltpu.roll(a, 64, 1), b).astype(BF)


def volume_call(rv, cells):
    cos, sin = dft_np()
    full = np.zeros((2, 256, 8, 2, 32))
    full[0, :, :, 0, :] = cos.reshape(256, 8, 32)
    full[1, :, :, 0, :] = -sin.reshape(256, 8, 32)
    full[0, :, :, 1, :] = sin.reshape(256, 8, 32)
    full[1, :, :, 1, :] = cos.reshape(256, 8, 32)
    dh, dl = split_np(full.reshape(512, 512))
    return pl.pallas_call(
        volume_kernel,
        out_shape=jax.ShapeDtypeStruct((8, 256, 128), BF),
        scratch_shapes=[pltpu.VMEM((1024, 256), F32)],
        compiler_params=pltpu.CompilerParams(vmem_limit_bytes=VMEM_LIMIT),
        name="volume_z",
    )(rv, cells, jnp.asarray(dh), jnp.asarray(dl))


def second_kernel(r1_ref, q_ref, dh_ref, dl_ref, out_ref):
    columns = []
    for xh in range(8):
        columns.append(jnp.concatenate([r1_ref[r, xh * 32:(xh + 1) * 32, :] for r in range(8)], axis=0))
    field = jnp.concatenate(columns, axis=1)
    turned = jnp.concatenate([dot(col, q_ref[...]).astype(BF) for col in columns], axis=1)
    both = jnp.concatenate([field, turned], axis=0)
    out = (dot(dh_ref[...], both) + dot(dl_ref[...], both)).astype(BF)
    for q in range(16):
        for xh in range(8):
            out_ref[q, xh] = out[q * 16:(q + 1) * 16, xh * 128:(xh + 1) * 128]


def second_call(r1):
    cos, sin = dft_np()
    dh, dl = split_np(np.concatenate([cos, sin], axis=1))
    turn = np.zeros((128, 128), np.float32)
    for g in range(2):
        for z in range(32):
            turn[g * 64 + 32 + z, g * 64 + z] = -1.0
            turn[g * 64 + z, g * 64 + 32 + z] = 1.0
    return pl.pallas_call(
        second_kernel,
        out_shape=jax.ShapeDtypeStruct((16, 8, 16, 128), BF),
        compiler_params=pltpu.CompilerParams(vmem_limit_bytes=VMEM_LIMIT),
        name="transform_y",
    )(r1, jnp.asarray(turn.astype(ml_dtypes.bfloat16)), jnp.asarray(dh), jnp.asarray(dl))


def third_kernel(r2_ref, dh_ref, dl_ref, out_ref, stage, lhs):
    stage[...] = r2_ref[...].astype(F32)
    for y in range(16):
        turned = jnp.transpose(stage[pl.ds(y, 128, stride=16), :])
        for g in range(4):
            lhs[g, pl.ds(y, 32, stride=16), :] = turned[g * 32:(g + 1) * 32, :]
    field = jnp.concatenate([lhs[g].astype(BF) for g in range(4)], axis=1)
    out = dot(field, dh_ref[...]) + dot(field, dl_ref[...])
    out_ref[0] = out[:, 0:256]
    out_ref[1] = out[:, 256:512]


def third_call(r2):
    cos, sin = dft_np()
    full = np.zeros((2, 2, 128, 2, 256))
    for xl in range(2):
        full[xl, 0, :, 0, :] = cos[xl::2]
        full[xl, 1, :, 0, :] = -sin[xl::2]
        full[xl, 0, :, 1, :] = sin[xl::2]
        full[xl, 1, :, 1, :] = cos[xl::2]
    dh, dl = split_np(full.reshape(512, 512))
    return pl.pallas_call(
        third_kernel,
        out_shape=jax.ShapeDtypeStruct((2, 512, 256), F32),
        scratch_shapes=[pltpu.VMEM((2048, 128), F32), pltpu.VMEM((4, 512, 128), F32)],
        compiler_params=pltpu.CompilerParams(vmem_limit_bytes=VMEM_LIMIT),
        name="transform_x",
    )(r2, jnp.asarray(dh), jnp.asarray(dl))


def by_rows(x):
    n = x.shape[0]
    return x.reshape(n, 2, 64, 128).transpose(0, 2, 1, 3).reshape(n, 128, 128)


def local(images, projections, noise_weight, shift_ids, owner_ids, cell_ids, weight_ids, interp_table):
    devices = lax.axis_size("img") * lax.axis_size("ori")
    n_ori = lax.axis_size("ori")
    n_slot = devices * CAP
    a, scores, stats = align_call(
        by_rows(images), by_rows(projections), noise_weight.reshape(64, 128), shift_ids, n_ori)
    all_stats = lax.all_to_all(stats, "ori", split_axis=0, concat_axis=0, tiled=True)
    weights = weight_ids.T

    def plan(*ready):
        owners = lax.optimization_barrier((owner_ids.T,) + ready)[0]
        return slots_call(owners, cell_ids.T, weights, n_slot)
    parts_a, parts_b, loglik, pos, slots, send_cells = reduce_slices(scores, all_stats, a, plan)
    loglik = loglik[:, :IB].reshape(-1)
    got_cells = lax.all_to_all(
        send_cells.reshape(devices, CAP), ("img", "ori"), split_axis=0, concat_axis=0, tiled=True)
    send = interp_call(parts_a, parts_b, weights, pos, slots, interp_table.reshape(-1, 128), n_slot)
    got = lax.all_to_all(
        send.reshape(devices, CAP, 256), ("img", "ori"), split_axis=0, concat_axis=0, tiled=True)
    first = volume_call(got.reshape(n_slot, 256), got_cells.reshape(1, n_slot))
    second = second_call(lax.all_to_all(first, "img", split_axis=0, concat_axis=0, tiled=True))
    third = lax.all_to_all(second, "ori", split_axis=0, concat_axis=0, tiled=True)
    realspace = third_call(third.reshape(2048, 128))
    return realspace.reshape(2, 32, 16, 256), loglik


def solution(mesh):
    placed = (
        P("img", None, None),
        P("ori", None, None),
        P(),
        P("img", None),
        P("ori", "img"),
        P("ori", "img"),
        P("ori", "img"),
        P(),
    )
    return jax.shard_map(
        local,
        mesh=mesh,
        in_specs=placed,
        out_specs=(P(None, "img", "ori", None), P("img")),
        check_vma=False,
    )
```

```python
import math
from functools import partial

import jax
import jax.numpy as jnp
import ml_dtypes
import numpy as np
from jax import lax
from jax.experimental import pallas as pl
from jax.experimental.pallas import tpu as pltpu
from jax.sharding import PartitionSpec as P

BF = jnp.bfloat16
F32 = jnp.float32
I32 = jnp.int32

IB = 64
PITCH = IB + 8
GR = 16
NA = 4
CAP = 24
VMEM_LIMIT = 56 * 1024 * 1024


def split_np(a):
    high = a.astype(ml_dtypes.bfloat16)
    low = (a - high.astype(np.float64)).astype(ml_dtypes.bfloat16)
    return high, low


def dft_np():
    k = np.arange(256)
    ang = 2.0 * math.pi * ((k[:, None] * k[None, :]) % 256) / 256.0
    return np.cos(ang) / 16.0, np.sin(ang) / 16.0


def dot(a, b):
    return lax.dot_general(a, b, (((1,), (0,)), ((), ())), preferred_element_type=F32)


def split(a):
    high = a.astype(BF)
    return high, (a - high.astype(F32)).astype(BF)


def align_kernel(x_ref, pr_ref, nw_ref, sh_ref, ex_ref, a_ref, sc_ref, st_ref,
                 xf, wk, pn, ph, stp, even, odd, sh):
    b = pl.program_id(0)

    def rows_of(r):
        return pl.ds(pl.multiple_of(r * PITCH, 8), IB)

    @pl.when(b == 0)
    def _():
        for k in range(sh.shape[0] // 128):
            ids = sh_ref[:, k * 128:(k + 1) * 128].astype(F32)
            sh[k * 128:(k + 1) * 128, :] = jnp.transpose(
                jnp.concatenate([ids, jnp.zeros((124, 128), F32)], axis=0))

        def chunk(oc, carry):
            for i in range(IB):
                xf[pl.ds(i, 128, stride=PITCH), :] = pr_ref[oc * IB + i].astype(F32)
            rows = pl.ds(pl.multiple_of(oc * IB, IB), IB)

            def ky_step(ky, acc):
                noise = nw_ref[pl.ds(ky, 1), :]
                for p in range(2):
                    v = xf[rows_of(2 * ky + p), :]
                    vn = v * noise
                    wk[rows, pl.ds(pl.multiple_of(ky * 256 + p * 128, 128), 128)] = vn.astype(BF)
                    acc = acc + v * vn
                return acc
            acc = lax.fori_loop(0, 64, ky_step, jnp.zeros((IB, 128), F32), unroll=4)
            pn[rows, :] = jnp.broadcast_to(jnp.sum(acc, axis=1, keepdims=True) * 0.5, (IB, 128))
            return carry
        lax.fori_loop(0, 128 // IB, chunk, 0)

    for i in range(IB):
        xf[pl.ds(i, 128, stride=PITCH), :] = x_ref[i].astype(F32)

    for s in range(4):
        t = sh[pl.ds(pl.multiple_of(b * IB, IB), IB), s:s + 1].astype(I32)
        ty = (t * 37) >> 8
        tx = t - ty * 7
        er = jnp.zeros((IB, 128), F32)
        ei = jnp.zeros((IB, 128), F32)
        sr = jnp.zeros((IB, 1), F32)
        si = jnp.zeros((IB, 1), F32)
        for d in range(7):
            hit = tx == d
            er = jnp.where(hit, ex_ref[d:d + 1, :], er)
            ei = jnp.where(hit, ex_ref[8 + d:9 + d, :], ei)
            ang = -2.0 * math.pi * (d - 3) / 128.0
            hity = ty == d
            sr = jnp.where(hity, math.cos(ang), sr)
            si = jnp.where(hity, math.sin(ang), si)
        ph[0, s] = er
        ph[1, s] = ei
        stp[0, s] = jnp.broadcast_to(sr, (IB, 128))
        stp[1, s] = jnp.broadcast_to(si, (IB, 128))

    def align_chunk(kc, buf):
        for s in range(4):
            for g in range(IB // GR):
                rows = slice(g * GR, (g + 1) * GR)
                pr = ph[0, s, rows]
                pi = ph[1, s, rows]
                sr = stp[0, s, rows]
                si = stp[1, s, rows]
                twice = sr + sr
                out = slice(s * IB + g * GR, s * IB + (g + 1) * GR)
                for j in range(8):
                    ky = kc * 8 + j
                    re = xf[pl.ds(pl.multiple_of(2 * ky * PITCH + g * GR, 8), GR), :]
                    im = xf[pl.ds(pl.multiple_of((2 * ky + 1) * PITCH + g * GR, 8), GR), :]
                    lane = pl.multiple_of(ky * 256, 256)
                    new_re = (re * pr - im * pi).astype(BF)
                    new_im = (re * pi + im * pr).astype(BF)
                    a_ref[out, pl.ds(lane, 128)] = new_re
                    a_ref[out, pl.ds(lane + 128, 128)] = new_im
                    buf[out, j * 256:j * 256 + 128] = new_re
                    buf[out, j * 256 + 128:j * 256 + 256] = new_im
                    if j == 0:
                        nr, ni = pr * sr - pi * si, pr * si + pi * sr
                    else:
                        nr, ni = twice * pr - lr, twice * pi - li
                    lr, li, pr, pi = pr, pi, nr, ni
                ph[0, s, rows] = pr
                ph[1, s, rows] = pi

    def score_chunk(kc, buf):
        lanes = pl.ds(pl.multiple_of(kc * 2048, 2048), 2048)
        return lax.dot_general(buf[...], wk[:, lanes], (((1,), (1,)), ((), ())),
                               preferred_element_type=F32)

    odd[...] = jnp.zeros_like(odd)

    def two_chunks(m, acc):
        acc = acc + score_chunk(jnp.maximum(2 * m - 1, 0), odd)
        align_chunk(2 * m, even)
        acc = acc + score_chunk(2 * m, even)
        align_chunk(2 * m + 1, odd)
        return acc
    acc = lax.fori_loop(0, 4, two_chunks, jnp.zeros((4 * IB, 128), F32))
    acc = acc + score_chunk(7, odd)
    sc = jnp.transpose(acc) - pn[:, 0:1]
    sc_ref[0] = sc
    mx = jnp.max(sc, axis=0, keepdims=True)
    if IB == 64:
        mx = jnp.maximum(mx[:, 0:128], mx[:, 128:256])
    mx = jnp.maximum(mx, pltpu.roll(mx, 64, 1))
    if IB == 32:
        mx = jnp.maximum(mx, pltpu.roll(mx, 32, 1))
    wide = jnp.concatenate([mx] * (IB // 32), axis=1)
    tot = jnp.sum(jnp.exp(sc - wide), axis=0, keepdims=True)
    if IB == 64:
        tot = tot[:, 0:128] + tot[:, 128:256]
    tot = tot + pltpu.roll(tot, 64, 1)
    if IB == 32:
        tot = tot + pltpu.roll(tot, 32, 1)
    for q in range(st_ref.shape[0]):
        st_ref[q, 0, pl.ds(b, 1), :] = mx
        st_ref[q, 1, pl.ds(b, 1), :] = tot


def align_call(xv, pv, noise, shifts, n_ori=16):
    n_img = xv.shape[0]
    steps = n_img // IB
    kx = np.arange(128) - 64
    ex = np.zeros((16, 128), np.float32)
    for d in range(7):
        ang = -2.0 * math.pi * ((kx * (d - 3)) % 128) / 128.0
        ex[d] = np.cos(ang)
        ex[8 + d] = np.sin(ang)
    whole3 = lambda b: (0, 0, 0)
    whole2 = lambda b: (0, 0)
    return pl.pallas_call(
        align_kernel,
        grid=(steps,),
        in_specs=[
            pl.BlockSpec((IB, 128, 128), lambda b: (b, 0, 0)),
            pl.BlockSpec((128, 128, 128), whole3, pipeline_mode=pl.Buffered(1)),
            pl.BlockSpec((64, 128), whole2),
            pl.BlockSpec((4, n_img), whole2),
            pl.BlockSpec((16, 128), whole2),
        ],
        out_specs=[
            pl.BlockSpec((4 * IB, 16384), lambda b: (b, 0)),
            pl.BlockSpec((1, 128, 4 * IB), lambda b: (b, 0, 0)),
            pl.BlockSpec((n_ori, 2, steps, 128), lambda b: (0, 0, 0, 0)),
        ],
        out_shape=[
            jax.ShapeDtypeStruct((4 * n_img, 16384), BF),
            jax.ShapeDtypeStruct((steps, 128, 4 * IB), F32),
            jax.ShapeDtypeStruct((n_ori, 2, steps, 128), F32),
        ],
        scratch_shapes=[
            pltpu.VMEM((128 * PITCH, 128), F32),
            pltpu.VMEM((128, 16384), BF),
            pltpu.VMEM((128, 128), F32),
            pltpu.VMEM((2, 4, IB, 128), F32),
            pltpu.VMEM((2, 4, IB, 128), F32),
            pltpu.VMEM((4 * IB, 2048), BF),
            pltpu.VMEM((4 * IB, 2048), BF),
            pltpu.VMEM((n_img, 128), F32),
        ],
        compiler_params=pltpu.CompilerParams(vmem_limit_bytes=VMEM_LIMIT),
        name="align_scores",
    )(xv, pv, noise, shifts, jnp.asarray(ex))


def prob_of(sc_ref, st_ref, ll_ref, pt):
    n = st_ref.shape[0]
    peak = st_ref[0, 0]
    for q in range(1, n):
        peak = jnp.maximum(peak, st_ref[q, 0])
    total = jnp.zeros_like(peak)
    for q in range(n):
        total = total + st_ref[q, 1] * jnp.exp(st_ref[q, 0] - peak)
    ll_ref[...] = peak + jnp.log(total)
    inv = 1.0 / total
    for blk in range(sc_ref.shape[0]):
        wide_peak = jnp.concatenate([peak[blk:blk + 1, :]] * (IB // 32), axis=1)
        wide_inv = jnp.concatenate([inv[blk:blk + 1, :]] * (IB // 32), axis=1)
        pr = jnp.exp(sc_ref[blk] - wide_peak) * wide_inv
        pt[:, blk * 4 * IB:(blk + 1) * 4 * IB] = pr.astype(BF)


def slices_call(dests, a, sizes, name, pt=None, sc=None, st=None):
    rows = a.shape[0]
    width = 256 * NA
    first = pt is None
    places = []
    for k, size in enumerate(sizes):
        places += [(k, None if size == 1 else m) for m in range(size)]
    n = len(places)

    def kernel(dest_ref, *refs):
        inputs = refs[:-2]
        buf, sem = refs[-2:]
        if first:
            sc_ref, st_ref, a_ref = inputs[:3]
            outs = inputs[3:]
            pt_ref, ll_ref = outs[len(sizes):]
        else:
            pt_ref, a_ref = inputs[:2]
            outs = inputs[2:]

        def copy(step):
            lanes = pl.ds(pl.multiple_of(dest_ref[step] * width, width), width)
            return pltpu.make_async_copy(a_ref.at[:, lanes], buf.at[step], sem.at[step])

        for step in range(n):
            copy(step).start()
        if first:
            prob_of(sc_ref, st_ref, ll_ref, pt_ref)
        for step, (k, m) in enumerate(places):
            copy(step).wait()
            res = dot(pt_ref[...], buf[step])
            for c in range(NA):
                piece = res[:, c * 256:(c + 1) * 256].astype(BF)
                if m is None:
                    outs[k][c] = piece
                else:
                    outs[k][m, c] = piece

    def keep(shape):
        return pl.BlockSpec(shape, lambda g, d: (0,) * len(shape))

    shapes = [(NA, 128, 256) if size == 1 else (size, NA, 128, 256) for size in sizes]
    out_shape = [jax.ShapeDtypeStruct(shape, BF) for shape in shapes]
    if first:
        inputs = [sc, st]
        out_shape += [jax.ShapeDtypeStruct((128, rows), BF), jax.ShapeDtypeStruct((sc.shape[0], 128), F32)]
    else:
        inputs = [pt]
    return pl.pallas_call(
        kernel,
        grid_spec=pltpu.PrefetchScalarGridSpec(
            num_scalar_prefetch=1,
            grid=(1,),
            in_specs=[keep(x.shape) for x in inputs] + [pl.BlockSpec(memory_space=pl.ANY)],
            out_specs=[keep(x.shape) for x in out_shape],
            scratch_shapes=[pltpu.VMEM((n, rows, width), BF), pltpu.SemaphoreType.DMA((n,))],
        ),
        out_shape=out_shape,
        compiler_params=pltpu.CompilerParams(vmem_limit_bytes=VMEM_LIMIT),
        name=name,
    )(dests, *inputs, a)


def added(*pieces):
    total = pieces[0].astype(F32)
    for piece in pieces[1:]:
        total = total + piece.astype(F32)
    return total.astype(BF)


def after(x, y):
    return lax.optimization_barrier((x, y))[0]


def reduce_slices(sc, st, a, plan):
    n_img = lax.axis_size("img")
    n_y = n_img // 2
    me = lax.axis_index("img")
    my_y = me >> 1
    my_z = me & 1

    def table(groups):
        return jnp.stack([
            (((my_y + dy) & (n_y - 1)) * 2 + ((my_z + dz) & 1)) * 2 + part for part, dy, dz in groups]).astype(I32)

    def shift_y(x, d):
        perm = [(y * 2 + z, ((y + d) % n_y) * 2 + z) for y in range(n_y) for z in range(2)]
        return lax.ppermute(x, "img", perm)

    def swap_z(x):
        return lax.ppermute(x, "img", [(i, i ^ 1) for i in range(n_img)])

    a20, a21, bz, pt, loglik = slices_call(
        table([(0, 2, 0), (0, 2, 1), (1, 2, 1), (1, 1, 1), (1, 3, 1), (1, 0, 1)]),
        a, (1, 1, 4), "slices_first", sc=sc, st=st)
    u = shift_y(a20, 1)
    v = shift_y(a21, -1)
    bz = swap_z(bz)
    to_left, to_right, b02, b01, b03, b00, a00, a01 = slices_call(
        table([(0, 1, 0), (0, 1, 1), (0, 3, 0), (0, 3, 1),
               (1, 2, 0), (1, 1, 0), (1, 3, 0), (1, 0, 0), (0, 0, 0), (0, 0, 1)]),
        a, (2, 2, 1, 1, 1, 1, 1, 1), "slices_rest", pt=pt)
    to_left = added(to_left, jnp.pad(u[None], ((0, 1), (0, 0), (0, 0), (0, 0))))
    to_right = added(to_right, jnp.pad(v[None], ((1, 0), (0, 0), (0, 0), (0, 0))))
    left = shift_y(to_left, 1)
    right = shift_y(to_right, -1)
    pos, slots, send_cells = plan(to_left, to_right)
    b02 = after(b02, pos)
    ub = shift_y(added(b02[:, :64], bz[0][:, :64]), 1)
    vb = shift_y(added(b02[:, 64:], bz[0][:, 64:]), -1)
    other = swap_z(added(a01, left[1], right[1]))
    left_b = shift_y(added(b01, bz[1], jnp.pad(ub, ((0, 0), (0, 64), (0, 0)))), 1)
    right_b = shift_y(added(b03, bz[2], jnp.pad(vb, ((0, 0), (64, 0), (0, 0)))), -1)
    return ((a00, left, right, other), (None, 0, 0, None)), ((b00, bz, left_b, right_b), (None, 3, None, None)), loglik, pos, slots, send_cells


def columns_of(rows8):
    return jnp.transpose(jnp.concatenate([rows8, jnp.zeros((120, 128), F32)], axis=0))


def two_parts(rows8, unit):
    high = jnp.floor(rows8 * (1.0 / unit))
    return high, rows8 - high * unit


def slots_kernel(ow_ref, ce_ref, wi_ref, pos_ref, slot_ref, cell_ref):
    lane = lax.broadcasted_iota(I32, (128, 128), 1)
    sub = lax.broadcasted_iota(I32, (128, 128), 0)
    lane_f = lane.astype(F32)
    lower = (sub >= lane).astype(F32).astype(BF)
    before = (sub < lane).astype(F32).astype(BF)
    owners = columns_of(ow_ref[...].astype(F32))
    weights = columns_of(wi_ref[...].astype(F32))
    base = jnp.zeros((1, 128), F32)
    base_w = jnp.zeros((1, 128), F32)
    slots = jnp.zeros((128, 128), F32)
    pos = jnp.zeros((128, 128), F32)
    slot_columns = []
    ranks = []
    for c in range(8):
        oc = owners[:, c:c + 1]
        hit = (oc == lane_f).astype(F32)
        run = dot(lower, hit.astype(BF)) + base
        rank = jnp.sum(run * hit, axis=1, keepdims=True) - 1.0
        base = base + jnp.sum(hit, axis=0, keepdims=True)
        slot = oc * float(CAP) + rank
        slot_columns.append(slot)
        slots = jnp.where(lane == c, slot, slots)
        hit = (weights[:, c:c + 1] == lane_f).astype(F32)
        run = dot(lower, hit.astype(BF)) + base_w
        ranks.append(jnp.sum(run * hit, axis=1, keepdims=True) - 1.0)
        base_w = base_w + jnp.sum(hit, axis=0, keepdims=True)
    high, low = two_parts(jnp.broadcast_to(base_w, (16, 128)), 32.0)
    start = (dot(high.astype(BF), before) * 32.0 + dot(low.astype(BF), before))[0:1, :]
    pos_columns = []
    for c in range(8):
        hit = weights[:, c:c + 1] == lane_f
        column = ranks[c] + jnp.sum(jnp.where(hit, start, 0.0), axis=1, keepdims=True)
        pos_columns.append(column)
        pos = jnp.where(lane == c, column, pos)
    pos_ref[...] = jnp.transpose(pos)[0:8, :].astype(I32)

    row = lax.broadcasted_iota(I32, (16, 128), 0)

    def scatter(parts_of, columns, n):
        to = lax.broadcasted_iota(I32, (128, n), 1).astype(F32)
        acc = jnp.zeros((16, n), F32)
        for c in range(8):
            high, low = parts_of(c)
            parts = jnp.where(row == 0, high, jnp.where(row == 1, low, jnp.where(row == 2, 1.0, 0.0)))
            acc = acc + dot(parts.astype(BF), (columns[c] == to).astype(F32).astype(BF))
        return acc

    slot_high, slot_low = two_parts(jnp.transpose(slots)[0:8, :], 64.0)
    acc = scatter(lambda c: (slot_high[c:c + 1, :], slot_low[c:c + 1, :]), pos_columns, 1024)
    slot_ref[...] = (acc[0:1, :] * 64.0 + acc[1:2, :]).astype(I32)
    cell_high, cell_low = two_parts(ce_ref[...].astype(F32), 32.0)
    acc = scatter(lambda c: (cell_high[c:c + 1, :], cell_low[c:c + 1, :]), slot_columns, cell_ref.shape[1])
    cell = acc[0:1, :] * 32.0 + acc[1:2, :]
    cell_ref[...] = jnp.where(acc[2:3, :] > 0.5, cell, -1.0).astype(I32)


def slots_call(owners, cells, weights, n_slot):
    return pl.pallas_call(
        slots_kernel,
        out_shape=[
            jax.ShapeDtypeStruct((8, 128), I32),
            jax.ShapeDtypeStruct((1, 1024), I32),
            jax.ShapeDtypeStruct((1, n_slot), I32),
        ],
        compiler_params=pltpu.CompilerParams(vmem_limit_bytes=VMEM_LIMIT),
        name="slots",
    )(owners, cells, weights)


WSTEP = 8
CHUNK = 128


def interp_kernel(picks, *refs):
    n_a, n_b = len(picks[0]), len(picks[1])
    parts = (refs[:n_a], refs[n_a:n_a + n_b])
    wi_ref, pos_ref, slot_ref, tab_ref, out_ref, raw, srt, con = refs[n_a + n_b:]
    weights = columns_of(wi_ref[...].astype(F32))
    for c in range(8):
        which, at = (0, c) if c < NA else (1, c - NA)
        total = jnp.zeros((128, 256), F32)
        for part, pick in zip(parts[which], picks[which]):
            total = total + (part[at] if pick is None else part[pick, at]).astype(F32)
        rows = slice(c * 128, (c + 1) * 128)
        raw[rows, 0:256] = total.astype(BF)
        raw[rows, 256:384] = jnp.broadcast_to(weights[:, c:c + 1], (128, 128)).astype(BF)

    def sort(k, carry):
        row = lax.broadcasted_iota(I32, (256, 128), 0) + k * 256
        pick = jnp.concatenate(
            [jnp.where(pos_ref[c:c + 1, :] == row, 1.0, 0.0).astype(BF) for c in range(8)], axis=1)
        srt[pl.ds(pl.multiple_of(k * 256, 256), 256), :] = dot(pick, raw[...]).astype(BF)
        return carry
    lax.fori_loop(0, 4, sort, 0)

    zero = jnp.zeros((CHUNK, 128), BF)

    def chunk(k, carry):
        rows = pl.ds(pl.multiple_of(k * CHUNK, CHUNK), CHUNK)
        ids = srt[rows, 256:384]
        ids_f = ids.astype(F32)
        lowest = jnp.min(ids_f[0:8, :]).astype(I32) // WSTEP
        highest = jnp.max(ids_f[CHUNK - 8:CHUNK, :]).astype(I32) // WSTEP

        def step(g, acc):
            pieces = []
            for p in range(2):
                values = srt[rows, p * 128:(p + 1) * 128]
                marks = [jnp.full((CHUNK, 128), (g * WSTEP + u).astype(F32), F32).astype(BF)
                         for u in range(WSTEP)]
                pieces.append(jnp.concatenate([jnp.where(ids == mark, values, zero) for mark in marks], axis=1))
            table = tab_ref[pl.ds(pl.multiple_of(g * (WSTEP * 128), WSTEP * 128), WSTEP * 128), :]
            return acc + dot(jnp.concatenate(pieces, axis=0), table)
        acc = lax.fori_loop(lowest, highest + 1, step, jnp.zeros((2 * CHUNK, 128), F32))
        con[rows, 0:128] = acc[0:CHUNK, :].astype(BF)
        con[rows, 128:256] = acc[CHUNK:, :].astype(BF)
        return carry
    lax.fori_loop(0, 1024 // CHUNK, chunk, 0)

    def place(k, carry):
        row = lax.broadcasted_iota(I32, (384, 1024), 0) + k * 384
        pick = jnp.where(slot_ref[...] == row, 1.0, 0.0).astype(BF)
        out_ref[pl.ds(pl.multiple_of(k * 384, 384), 384), :] = dot(pick, con[...]).astype(BF)
        return carry
    lax.fori_loop(0, out_ref.shape[0] // 384, place, 0)


def interp_call(parts_a, parts_b, weights, pos, slots, table, n_slot):
    return pl.pallas_call(
        partial(interp_kernel, (parts_a[1], parts_b[1])),
        out_shape=jax.ShapeDtypeStruct((n_slot, 256), BF),
        scratch_shapes=[
            pltpu.VMEM((1024, 384), BF),
            pltpu.VMEM((1024, 384), BF),
            pltpu.VMEM((1024, 256), BF),
        ],
        compiler_params=pltpu.CompilerParams(vmem_limit_bytes=VMEM_LIMIT),
        name="interpolate",
    )(*parts_a[0], *parts_b[0], weights, pos, slots, table)


def volume_kernel(rv_ref, cell_ref, dh_ref, dl_ref, out_ref, vol):
    n_slot = rv_ref.shape[0]
    cell = cell_ref[...]
    half = cell & 1
    y = (cell >> 1) & 31
    x = cell >> 6
    where = half * 512 + (x & 1) * 256 + (x >> 1) * 32 + y
    where = jnp.where(cell < 0, -1, where)

    def land(k, carry):
        row = lax.broadcasted_iota(I32, (128, n_slot), 0) + k * 128
        pick = jnp.where(where == row, 1.0, 0.0).astype(BF)
        vol[pl.ds(pl.multiple_of(k * 128, 128), 128), :] = dot(pick, rv_ref[...])
        return carry
    lax.fori_loop(0, 8, land, 0)
    lane = lax.broadcasted_iota(I32, (256, 128), 1)
    outs = []
    for xl in range(2):
        lo = slice(xl * 256, (xl + 1) * 256)
        hi = slice(512 + xl * 256, 512 + (xl + 1) * 256)
        field = jnp.concatenate(
            [vol[lo, 0:128], vol[hi, 0:128], vol[lo, 128:256], vol[hi, 128:256]], axis=1)
        fh, fl = split(field)
        outs.append(dot(fh, dh_ref[...]) + dot(fl, dh_ref[...]) + dot(fh, dl_ref[...]))
    for t in range(4):
        a = outs[0][:, t * 128:(t + 1) * 128]
        b = outs[1][:, t * 128:(t + 1) * 128]
        out_ref[2 * t] = jnp.where(lane < 64, a, pltpu.roll(b, 64, 1)).astype(BF)
        out_ref[2 * t + 1] = jnp.where(lane < 64, pltpu.roll(a, 64, 1), b).astype(BF)


def volume_call(rv, cells):
    cos, sin = dft_np()
    full = np.zeros((2, 256, 8, 2, 32))
    full[0, :, :, 0, :] = cos.reshape(256, 8, 32)
    full[1, :, :, 0, :] = -sin.reshape(256, 8, 32)
    full[0, :, :, 1, :] = sin.reshape(256, 8, 32)
    full[1, :, :, 1, :] = cos.reshape(256, 8, 32)
    dh, dl = split_np(full.reshape(512, 512))
    return pl.pallas_call(
        volume_kernel,
        out_shape=jax.ShapeDtypeStruct((8, 256, 128), BF),
        scratch_shapes=[pltpu.VMEM((1024, 256), F32)],
        compiler_params=pltpu.CompilerParams(vmem_limit_bytes=VMEM_LIMIT),
        name="volume_z",
    )(rv, cells, jnp.asarray(dh), jnp.asarray(dl))


def second_kernel(r1_ref, q_ref, dh_ref, dl_ref, out_ref):
    columns = []
    for xh in range(8):
        columns.append(jnp.concatenate([r1_ref[r, xh * 32:(xh + 1) * 32, :] for r in range(8)], axis=0))
    field = jnp.concatenate(columns, axis=1)
    turned = jnp.concatenate([dot(col, q_ref[...]).astype(BF) for col in columns], axis=1)
    both = jnp.concatenate([field, turned], axis=0)
    out = (dot(dh_ref[...], both) + dot(dl_ref[...], both)).astype(BF)
    for q in range(16):
        for xh in range(8):
            out_ref[q, xh] = out[q * 16:(q + 1) * 16, xh * 128:(xh + 1) * 128]


def second_call(r1):
    cos, sin = dft_np()
    dh, dl = split_np(np.concatenate([cos, sin], axis=1))
    turn = np.zeros((128, 128), np.float32)
    for g in range(2):
        for z in range(32):
            turn[g * 64 + 32 + z, g * 64 + z] = -1.0
            turn[g * 64 + z, g * 64 + 32 + z] = 1.0
    return pl.pallas_call(
        second_kernel,
        out_shape=jax.ShapeDtypeStruct((16, 8, 16, 128), BF),
        compiler_params=pltpu.CompilerParams(vmem_limit_bytes=VMEM_LIMIT),
        name="transform_y",
    )(r1, jnp.asarray(turn.astype(ml_dtypes.bfloat16)), jnp.asarray(dh), jnp.asarray(dl))


def third_kernel(r2_ref, dh_ref, dl_ref, out_ref, stage, lhs):
    stage[...] = r2_ref[...].astype(F32)
    for y in range(16):
        turned = jnp.transpose(stage[pl.ds(y, 128, stride=16), :])
        for g in range(4):
            lhs[g, pl.ds(y, 32, stride=16), :] = turned[g * 32:(g + 1) * 32, :]
    field = jnp.concatenate([lhs[g].astype(BF) for g in range(4)], axis=1)
    out = dot(field, dh_ref[...]) + dot(field, dl_ref[...])
    out_ref[0] = out[:, 0:256]
    out_ref[1] = out[:, 256:512]


def third_call(r2):
    cos, sin = dft_np()
    full = np.zeros((2, 2, 128, 2, 256))
    for xl in range(2):
        full[xl, 0, :, 0, :] = cos[xl::2]
        full[xl, 1, :, 0, :] = -sin[xl::2]
        full[xl, 0, :, 1, :] = sin[xl::2]
        full[xl, 1, :, 1, :] = cos[xl::2]
    dh, dl = split_np(full.reshape(512, 512))
    return pl.pallas_call(
        third_kernel,
        out_shape=jax.ShapeDtypeStruct((2, 512, 256), F32),
        scratch_shapes=[pltpu.VMEM((2048, 128), F32), pltpu.VMEM((4, 512, 128), F32)],
        compiler_params=pltpu.CompilerParams(vmem_limit_bytes=VMEM_LIMIT),
        name="transform_x",
    )(r2, jnp.asarray(dh), jnp.asarray(dl))


def by_rows(x):
    n = x.shape[0]
    return x.reshape(n, 2, 64, 128).transpose(0, 2, 1, 3).reshape(n, 128, 128)


def local(images, projections, noise_weight, shift_ids, owner_ids, cell_ids, weight_ids, interp_table):
    devices = lax.axis_size("img") * lax.axis_size("ori")
    n_ori = lax.axis_size("ori")
    n_slot = devices * CAP
    a, scores, stats = align_call(
        by_rows(images), by_rows(projections), noise_weight.reshape(64, 128), shift_ids.T, n_ori)
    all_stats = lax.all_to_all(stats, "ori", split_axis=0, concat_axis=0, tiled=True)
    weights = weight_ids.T

    def plan(*ready):
        owners = lax.optimization_barrier((owner_ids.T,) + ready)[0]
        return slots_call(owners, cell_ids.T, weights, n_slot)
    parts_a, parts_b, loglik, pos, slots, send_cells = reduce_slices(scores, all_stats, a, plan)
    loglik = loglik[:, :IB].reshape(-1)
    got_cells = lax.all_to_all(
        send_cells.reshape(devices, CAP), ("img", "ori"), split_axis=0, concat_axis=0, tiled=True)
    send = interp_call(parts_a, parts_b, weights, pos, slots, interp_table.reshape(-1, 128), n_slot)
    got = lax.all_to_all(
        send.reshape(devices, CAP, 256), ("img", "ori"), split_axis=0, concat_axis=0, tiled=True)
    first = volume_call(got.reshape(n_slot, 256), got_cells.reshape(1, n_slot))
    second = second_call(lax.all_to_all(first, "img", split_axis=0, concat_axis=0, tiled=True))
    third = lax.all_to_all(second, "ori", split_axis=0, concat_axis=0, tiled=True)
    realspace = third_call(third.reshape(2048, 128))
    return realspace.reshape(2, 32, 16, 256), loglik


def solution(mesh):
    placed = (
        P("img", None, None),
        P("ori", None, None),
        P(),
        P("img", None),
        P("ori", "img"),
        P("ori", "img"),
        P("ori", "img"),
        P(),
    )
    return jax.shard_map(
        local,
        mesh=mesh,
        in_specs=placed,
        out_specs=(P(None, "img", "ori", None), P("img")),
        check_vma=False,
    )
```
